128 devices in a mesh: tm: 8 (over y, core), height: 16 (over z, x).
Axes of the slice: x: 4, y: 4, z: 4, core: 2. Of those that a mesh axis runs over, the one named last changes fastest.
Arguments:
- queries: bfloat16 [8, 16, 2, 64, 3072], P('tm', 'height'), may hold values from -40 to 40
- keys_values: bfloat16 [8, 16, 2, 2, 64, 3072], P('tm', 'height'), may hold values from -6.2 to 6.2
- far_cubes: int32 [8, 16, 2, 24, 16], P('tm', 'height'), may hold values from 0 to 255, as said below
- out_weight: bfloat16 [3072, 3072], replicated, may hold values from -0.59765625 to 0.59765625
Outputs:
- output: bfloat16 [8, 16, 2, 64, 3072], P('tm', 'height')
The draws below stay inside these ranges and needn't reach their ends.
Inputs may be any that keep to these rules, and one draw needn't show every extreme that they name: `far_cubes`: the 16 cubes of one list are distinct. Over all cubes that one device holds, the distinct pairs (far cube, head) whose cube lies on one given device number at most 4, and exactly 4 for some given devices, from every device.
All inputs are finite; a program needn't handle non-finite values.
Results may differ from the reference program's by a relative error of at most 0.0058.
Values may be sent and summed in bfloat16 or wider, within the bound.
A program may use at most 256 MiB of HBM per device.

```python
import math
import jax
import jax.numpy as jnp
from jax import lax

HEADS = 24
HEAD_DIM = 128
D = 3072
CUBE = 64
FAR = 16
SLOTS = 512
CT = 1
CH = 1
NW = 2
N_TM = 8
N_HEIGHT = 16


def attention_fields(key):
    key = jax.random.fold_in(key, 11)
    key_query, key_field = jax.random.split(key)
    grid_time = CT * N_TM
    grid_height = CH * N_HEIGHT
    width = HEADS * HEAD_DIM
    query_shape = (grid_time, grid_height, NW, CUBE, width)
    field_shape = (grid_time, grid_height, NW, 2, CUBE, width)
    queries = jnp.clip(jax.random.normal(key_query, query_shape, jnp.float32) * 2.0, -12.0, 12.0)
    fields = jnp.clip(jax.random.normal(key_field, field_shape, jnp.float32), -6.0, 6.0)
    return (queries, fields)


def draw_queries(key, part):
    return attention_fields(key)[0].astype(jnp.bfloat16)


def draw_keys_values(key, part):
    return attention_fields(key)[1].astype(jnp.bfloat16)


def draw_far_cubes(key, part):
    key = jax.random.fold_in(key, 23)
    key_order, key_cube, key_hot, key_score = jax.random.split(key, 4)
    devices = N_TM * N_HEIGHT
    capacity = SLOTS // devices
    local = CT * CH * NW
    hot_count = 4
    grid_height = CH * N_HEIGHT
    orders = jax.vmap(lambda single: jax.random.permutation(single, devices))(jax.random.split(key_order, devices))
    slot_head = (orders[:, :, None] % HEADS + jnp.arange(capacity, dtype=jnp.int32)[None, None, :]) % HEADS
    slot_head = slot_head.reshape(devices, SLOTS)
    slot_cube = jax.random.randint(key_cube, (devices, SLOTS), 0, local, dtype=jnp.int32)
    hot_owners = jax.random.permutation(key_hot, devices)[:hot_count]
    slot_owner = jnp.arange(SLOTS, dtype=jnp.int32) // capacity
    hot_slot = jnp.any(slot_owner[:, None] == hot_owners[None, :], axis=1)
    noise = jax.random.randint(key_score, (devices, local, HEADS, SLOTS), 0, 2 ** 19, dtype=jnp.int32)
    score = noise * SLOTS + jnp.arange(SLOTS, dtype=jnp.int32)[None, None, None, :]
    score = score + jnp.where(hot_slot, 2 ** 30, 0).astype(jnp.int32)[None, None, None, :]
    matching = slot_head[:, None, None, :] == jnp.arange(HEADS, dtype=jnp.int32)[None, None, :, None]
    score = jnp.where(matching, score, -1)
    picked = lax.top_k(score, FAR)[1].astype(jnp.int32)
    owner = picked // capacity
    cube_local = jnp.take_along_axis(jnp.broadcast_to(slot_cube[:, None, None, :], score.shape), picked, axis=-1)
    owner_time = owner // N_HEIGHT
    owner_height = owner % N_HEIGHT
    local_time = cube_local // (CH * NW)
    local_height = cube_local // NW % CH
    local_width = cube_local % NW
    global_time = owner_time * CT + local_time
    global_height = owner_height * CH + local_height
    numbers = (global_time * grid_height + global_height) * NW + local_width
    numbers = numbers.reshape(N_TM, N_HEIGHT, CT, CH, NW, HEADS, FAR)
    numbers = jnp.transpose(numbers, (0, 2, 1, 3, 4, 5, 6))
    return numbers.reshape(CT * N_TM, grid_height, NW, HEADS, FAR).astype(jnp.int32)


def centred(key, dims, scale, reach, held_as=jnp.bfloat16):
    result = jax.random.normal(key, dims, jnp.float32) * scale
    return jnp.minimum(jnp.maximum(result, -reach), reach).astype(held_as)


def setup_inputs(seed: int = 0) -> dict:
    splits = jax.random.split(jax.random.key(seed), 5)
    return {
        "queries": draw_queries(jax.random.fold_in(splits[4], 71), 0),
        "keys_values": draw_keys_values(jax.random.fold_in(splits[4], 71), 0),
        "far_cubes": draw_far_cubes(jax.random.fold_in(splits[4], 71), 0),
        "out_weight": centred(splits[3], (D, D), 0.1, 0.59765625),
    }


def reference(queries, keys_values, far_cubes, out_weight):
    heads = HEADS
    head_size = HEAD_DIM
    grid_time = CT * N_TM
    grid_height = CH * N_HEIGHT
    grid_width = NW
    cube_count = grid_time * grid_height * grid_width
    width = heads * head_size
    padded = jnp.pad(keys_values, ((1, 1), (1, 1), (1, 1), (0, 0), (0, 0), (0, 0)))
    flat_queries = queries.reshape(cube_count, CUBE, heads, head_size)
    flat_fields = keys_values.reshape(cube_count, 2, CUBE, heads, head_size)
    flat_far = far_cubes.reshape(cube_count, heads, FAR)
    offsets = jnp.arange(3, dtype=jnp.int32) - 1
    head_index = jnp.arange(heads, dtype=jnp.int32)
    scale = 1.0 / math.sqrt(head_size)
    zero = jnp.zeros((), jnp.int32)

    def one_cube(index):
        time_pos = (index // (grid_height * grid_width)).astype(jnp.int32)
        height_pos = (index // grid_width % grid_height).astype(jnp.int32)
        width_pos = (index % grid_width).astype(jnp.int32)
        window = lax.dynamic_slice(padded, (time_pos, height_pos, width_pos, zero, zero, zero), (3, 3, 3, 2, CUBE, width))
        window = window.reshape(27, 2, CUBE, heads, head_size)
        inside_time = (time_pos + offsets >= 0) & (time_pos + offsets < grid_time)
        inside_height = (height_pos + offsets >= 0) & (height_pos + offsets < grid_height)
        inside_width = (width_pos + offsets >= 0) & (width_pos + offsets < grid_width)
        valid = (inside_time[:, None, None] & inside_height[None, :, None] & inside_width[None, None, :]).reshape(27)
        keys_window = window[:, 0].reshape(27 * CUBE, heads, head_size).astype(jnp.float32)
        values_window = window[:, 1].reshape(27 * CUBE, heads, head_size).astype(jnp.float32)
        far_tiles = flat_fields[flat_far[index], :, :, head_index[:, None], :]
        query = flat_queries[index].astype(jnp.float32)
        score_window = jnp.einsum('qhd,khd->hqk', query, keys_window) * scale
        score_window = jnp.where(jnp.repeat(valid, CUBE)[None, None, :], score_window, -jnp.inf)
        score_far = jnp.einsum('qhd,hfkd->hqfk', query, far_tiles[:, :, 0].astype(jnp.float32)) * scale
        scores = jnp.concatenate([score_window, score_far.reshape(heads, CUBE, FAR * CUBE)], axis=-1)
        largest = lax.optimization_barrier(jnp.max(scores, axis=-1, keepdims=True))
        lifted = jnp.exp(scores - largest)
        weights = (lifted / lax.optimization_barrier(jnp.sum(lifted, axis=-1, keepdims=True))).astype(jnp.bfloat16)
        weights = lax.optimization_barrier(weights).astype(jnp.float32)
        attended = jnp.einsum('hqk,khd->qhd', weights[:, :, :27 * CUBE], values_window)
        far_weights = weights[:, :, 27 * CUBE:].reshape(heads, CUBE, FAR, CUBE)
        attended = attended + jnp.einsum('hqfk,hfkd->qhd', far_weights, far_tiles[:, :, 1].astype(jnp.float32))
        return attended.reshape(CUBE, width).astype(jnp.bfloat16)
    attended = lax.map(one_cube, jnp.arange(cube_count, dtype=jnp.int32))
    output = jnp.dot(attended.reshape(cube_count * CUBE, width), out_weight, preferred_element_type=jnp.float32)
    return output.astype(jnp.bfloat16).reshape(queries.shape)
```

```python
import functools
import math

import jax
import jax.numpy as jnp
from jax import lax
from jax.experimental import pallas as pl
from jax.experimental.pallas import tpu as pltpu
from jax.sharding import PartitionSpec as P

HEADS = 24
HEAD_DIM = 128
CUBE = 64
FAR = 16
NW = 2
SLOTS = 512
PAIR = 2
ROWS = NW * CUBE
NEG = -1e30
EXP2_SCALE = math.log2(math.e) / math.sqrt(HEAD_DIM)


def request_tables(far, device_count):
    capacity = SLOTS // device_count
    cubes = device_count * NW
    hit = far[:, :, :, None] == jnp.arange(cubes, dtype=jnp.int32)
    wanted = jnp.any(hit, axis=(0, 2))
    wanted = jnp.transpose(wanted.reshape(HEADS, device_count, NW), (1, 2, 0))
    wanted = wanted.reshape(device_count, NW * HEADS)
    codes = jnp.arange(NW * HEADS, dtype=jnp.int32)
    before = (codes[:, None] < codes[None, :]).astype(jnp.bfloat16)
    rank = jnp.dot(wanted.astype(jnp.bfloat16), before, preferred_element_type=jnp.float32)
    rank = rank.astype(jnp.int32)
    chosen = wanted[:, :, None] & (rank[:, :, None] == jnp.arange(capacity, dtype=jnp.int32))
    requests = jnp.sum(jnp.where(chosen, codes[None, :, None], 0), axis=1)
    slot = rank + jnp.arange(device_count, dtype=jnp.int32)[:, None] * capacity
    slot = jnp.transpose(slot.reshape(device_count, NW, HEADS), (2, 0, 1)).reshape(HEADS, cubes)
    far_slot = jnp.sum(jnp.where(hit, slot[None, :, None, :], 0), axis=-1)
    return requests, far_slot


def gather_kernel(asked_ref, kv_ref, out_ref, sem):
    def start(i, carry):
        code = asked_ref[i]
        lane = pl.multiple_of(code % HEADS * HEAD_DIM, HEAD_DIM)
        pltpu.make_async_copy(
            kv_ref.at[code // HEADS, :, :, pl.ds(lane, HEAD_DIM)], out_ref.at[i], sem
        ).start()
        return carry

    lax.fori_loop(0, SLOTS, start, 0)
    pltpu.make_async_copy(out_ref, out_ref, sem).wait()


def gather_tiles(asked, kv):
    return pl.pallas_call(
        gather_kernel,
        name="gather_tiles",
        out_shape=jax.ShapeDtypeStruct((SLOTS, 2, CUBE, HEAD_DIM), kv.dtype),
        grid_spec=pltpu.PrefetchScalarGridSpec(
            num_scalar_prefetch=1,
            grid=(1,),
            in_specs=[pl.BlockSpec(kv.shape, lambda i, a: (0, 0, 0, 0))],
            out_specs=pl.BlockSpec(memory_space=pl.ANY),
            scratch_shapes=[pltpu.SemaphoreType.DMA],
        ),
        cost_estimate=pl.CostEstimate(
            flops=0, bytes_accessed=2 * SLOTS * 2 * CUBE * HEAD_DIM, transcendentals=0
        ),
    )(asked, kv)


def window_kernel(valid_ref, q_ref, *refs):
    blocks, (acc_ref, stat_ref) = refs[:9], refs[9:]
    for p in range(PAIR):
        lanes = slice(p * HEAD_DIM, (p + 1) * HEAD_DIM)
        query = q_ref[:, lanes]
        parts = []
        for j in range(9):
            keys = blocks[j][:, 0, :, lanes].reshape(ROWS, HEAD_DIM)
            score = lax.dot_general(
                query, keys, (((1,), (1,)), ((), ())), preferred_element_type=jnp.float32
            )
            parts.append(jnp.where(valid_ref[j] > 0, score, NEG))
        scores = jnp.concatenate(parts, axis=-1)
        largest = jnp.max(scores, axis=-1, keepdims=True)
        lifted = jnp.exp2((scores - largest) * EXP2_SCALE)
        total = jnp.sum(lifted, axis=-1, keepdims=True)
        values = jnp.concatenate(
            [blocks[j][:, 1, :, lanes].reshape(ROWS, HEAD_DIM) for j in range(9)], axis=0
        )
        acc_ref[p] = jnp.dot(
            lifted.astype(jnp.bfloat16), values, preferred_element_type=jnp.float32
        )
        lane = lax.broadcasted_iota(jnp.int32, (ROWS, HEAD_DIM), 1)
        stat_ref[p] = jnp.where(lane < HEAD_DIM // 2, largest, total)


def window_attention(valid, queries, blocks):
    steps = HEADS // PAIR
    width = PAIR * HEAD_DIM
    stat = jax.ShapeDtypeStruct((HEADS, ROWS, HEAD_DIM), jnp.float32)
    block = pl.BlockSpec((NW, 2, CUBE, width), lambda i, v: (0, 0, 0, i))
    out = pl.BlockSpec((PAIR, ROWS, HEAD_DIM), lambda i, v: (i, 0, 0))
    return pl.pallas_call(
        window_kernel,
        name="window_attention",
        out_shape=(stat, stat),
        grid_spec=pltpu.PrefetchScalarGridSpec(
            num_scalar_prefetch=1,
            grid=(steps,),
            in_specs=[pl.BlockSpec((ROWS, width), lambda i, v: (0, i))] + [block] * 9,
            out_specs=(out, out),
        ),
        cost_estimate=pl.CostEstimate(
            flops=HEADS * 4 * ROWS * 9 * ROWS * HEAD_DIM,
            bytes_accessed=20_000_000,
            transcendentals=HEADS * ROWS * 9 * ROWS,
        ),
    )(valid, queries, *blocks)


def far_kernel(
    slot_ref, q_ref, tiles_ref, acc_ref, stat_ref, w_ref, out_ref, buf, total, sem
):
    step = pl.program_id(0)
    steps = pl.num_programs(0)
    lists = PAIR * NW

    def fetch(at, into):
        def start(i, carry):
            head = at * PAIR + i // (NW * FAR)
            cube = i // FAR % NW
            slot = slot_ref[(cube * HEADS + head) * FAR + i % FAR]
            pltpu.make_async_copy(
                tiles_ref.at[slot], buf.at[into, i // FAR, i % FAR], sem.at[into]
            ).start()
            return carry

        lax.fori_loop(0, lists * FAR, start, 0)

    @pl.when(step == 0)
    def _():
        fetch(0, 0)
        total[...] = jnp.zeros_like(total)

    now = step % 2

    @pl.when(step + 1 < steps)
    def _():
        fetch(step + 1, 1 - now)

    pltpu.make_async_copy(buf.at[now], buf.at[now], sem.at[now]).wait()
    heads = []
    for p in range(PAIR):
        cubes = []
        for c in range(NW):
            rows = slice(c * CUBE, (c + 1) * CUBE)
            query = q_ref[rows, p * HEAD_DIM : (p + 1) * HEAD_DIM]
            keys = buf[now, p * NW + c, :, 0].reshape(FAR * CUBE, HEAD_DIM)
            values = buf[now, p * NW + c, :, 1].reshape(FAR * CUBE, HEAD_DIM)
            scores = lax.dot_general(
                query, keys, (((1,), (1,)), ((), ())), preferred_element_type=jnp.float32
            )
            near_max = stat_ref[p, rows, 0:1]
            near_sum = stat_ref[p, rows, HEAD_DIM // 2 : HEAD_DIM // 2 + 1]
            largest = jnp.maximum(near_max, jnp.max(scores, axis=-1, keepdims=True))
            lifted = jnp.exp2((scores - largest) * EXP2_SCALE)
            fade = jnp.exp2((near_max - largest) * EXP2_SCALE)
            weight = near_sum * fade + jnp.sum(lifted, axis=-1, keepdims=True)
            summed = acc_ref[p, rows] * fade + jnp.dot(
                lifted.astype(jnp.bfloat16), values, preferred_element_type=jnp.float32
            )
            cubes.append((summed / weight).astype(jnp.bfloat16))
        heads.append(jnp.concatenate(cubes, axis=0))
    attended = jnp.concatenate(heads, axis=1)
    total[...] += jnp.dot(attended, w_ref[...], preferred_element_type=jnp.float32)

    @pl.when(step == steps - 1)
    def _():
        out_ref[...] = total[...].astype(out_ref.dtype)


def far_attention(far_slot, queries, tiles, acc, stat, out_weight):
    steps = HEADS // PAIR
    width = PAIR * HEAD_DIM
    model = queries.shape[1]
    near = pl.BlockSpec((PAIR, ROWS, HEAD_DIM), lambda i, s: (i, 0, 0))
    return pl.pallas_call(
        far_kernel,
        name="far_attention",
        out_shape=jax.ShapeDtypeStruct((ROWS, model), queries.dtype),
        grid_spec=pltpu.PrefetchScalarGridSpec(
            num_scalar_prefetch=1,
            grid=(steps,),
            in_specs=[
                pl.BlockSpec((ROWS, width), lambda i, s: (0, i)),
                pl.BlockSpec(memory_space=pl.ANY),
                near,
                near,
                pl.BlockSpec((width, model), lambda i, s: (i, 0)),
            ],
            out_specs=pl.BlockSpec((ROWS, model), lambda i, s: (0, 0)),
            scratch_shapes=[
                pltpu.VMEM((2, PAIR * NW, FAR, 2, CUBE, HEAD_DIM), queries.dtype),
                pltpu.VMEM((ROWS, model), jnp.float32),
                pltpu.SemaphoreType.DMA((2,)),
            ],
        ),
        cost_estimate=pl.CostEstimate(
            flops=HEADS * 4 * ROWS * FAR * CUBE * HEAD_DIM + 2 * ROWS * model * model,
            bytes_accessed=50_000_000,
            transcendentals=HEADS * ROWS * FAR * CUBE,
        ),
    )(far_slot, queries, tiles, acc, stat, out_weight)


def body(queries, keys_values, far_cubes, out_weight):
    tm_count = lax.axis_size("tm")
    height_count = lax.axis_size("height")
    device_count = tm_count * height_count
    model = queries.shape[-1]
    far = far_cubes.reshape(NW, HEADS, FAR)
    requests, far_slot = request_tables(far, device_count)
    asked = lax.all_to_all(requests, ("tm", "height"), split_axis=0, concat_axis=0, tiled=True)
    kv = keys_values.reshape(NW, 2, CUBE, model)
    tiles = gather_tiles(asked.reshape(SLOTS), kv)
    tiles = lax.all_to_all(tiles, ("tm", "height"), split_axis=0, concat_axis=0, tiled=True)

    def ring(axis, count, by):
        return [(i, (i + by) % count) for i in range(count)]

    column = [
        lax.ppermute(kv, "height", ring("height", height_count, 1)),
        kv,
        lax.ppermute(kv, "height", ring("height", height_count, -1)),
    ]
    blocks = [lax.ppermute(b, "tm", ring("tm", tm_count, 1)) for b in column]
    blocks = blocks + column
    blocks = blocks + [lax.ppermute(b, "tm", ring("tm", tm_count, -1)) for b in column]
    offsets = jnp.arange(3, dtype=jnp.int32) - 1
    times = lax.axis_index("tm") + offsets
    heights = lax.axis_index("height") + offsets
    valid = ((times >= 0) & (times < tm_count))[:, None]
    valid = valid & ((heights >= 0) & (heights < height_count))[None, :]
    valid = valid.reshape(9).astype(jnp.int32)
    flat_queries = queries.reshape(ROWS, model)
    acc, stat = window_attention(valid, flat_queries, blocks)
    output = far_attention(
        far_slot.reshape(NW * HEADS * FAR), flat_queries, tiles, acc, stat, out_weight
    )
    return output.reshape(queries.shape)


def solution(mesh):
    in_specs = (
        P("tm", "height", None, None, None),
        P("tm", "height", None, None, None, None),
        P("tm", "height", None, None, None),
        P(),
    )
    out_specs = P("tm", "height", None, None, None)
    return jax.shard_map(body, mesh=mesh, in_specs=in_specs, out_specs=out_specs, check_vma=False)
```

```python
import functools
import math

import jax
import jax.numpy as jnp
from jax import lax
from jax.experimental import pallas as pl
from jax.experimental.pallas import tpu as pltpu
from jax.sharding import PartitionSpec as P

HEADS = 24
HEAD_DIM = 128
CUBE = 64
FAR = 16
NW = 2
SLOTS = 512
PAIR = 2
ROWS = NW * CUBE
NEG = -1e30
EXP2_SCALE = math.log2(math.e) / math.sqrt(HEAD_DIM)


def request_tables(far, device_count):
    capacity = SLOTS // device_count
    cubes = device_count * NW
    hit = far[:, :, :, None] == jnp.arange(cubes, dtype=jnp.int32)
    wanted = jnp.any(hit, axis=(0, 2))
    wanted = jnp.transpose(wanted.reshape(HEADS, device_count, NW), (1, 2, 0))
    wanted = wanted.reshape(device_count, NW * HEADS)
    codes = jnp.arange(NW * HEADS, dtype=jnp.int32)
    before = (codes[:, None] < codes[None, :]).astype(jnp.bfloat16)
    rank = jnp.dot(wanted.astype(jnp.bfloat16), before, preferred_element_type=jnp.float32)
    rank = rank.astype(jnp.int32)
    chosen = wanted[:, :, None] & (rank[:, :, None] == jnp.arange(2 * capacity, dtype=jnp.int32))
    labels = codes // HEADS * 32 + codes % HEADS
    requests = jnp.sum(jnp.where(chosen, labels[None, :, None], 0), axis=1)
    slot = rank + jnp.arange(device_count, dtype=jnp.int32)[:, None] * capacity
    slot = jnp.transpose(slot.reshape(device_count, NW, HEADS), (2, 0, 1)).reshape(HEADS, cubes)
    far_slot = jnp.sum(jnp.where(hit, slot[None, :, None, :], 0), axis=-1)
    rank, owner = far_slot % capacity, far_slot // capacity
    y, k, z, x = owner // 32, owner // 16 % 2, owner // 4 % 4, owner % 4
    in_x = (((y * 4 + z) * 2 + k) * 4 + x) * capacity + rank
    in_y = (((z * 4 + x) * 2 + k) * 4 + y) * capacity + rank
    in_z = (((x * 4 + y) * 2 + k) * 4 + z) * capacity + rank
    return requests.T, in_x + in_y * SLOTS + in_z * SLOTS * SLOTS


PART_ROWS = (48, 48, 32)
PIECES = (
    ((0, 0, 48, 0),),
    ((0, 48, 64, 0), (1, 0, 32, 16)),
    ((1, 32, 64, 0),),
)
AXES = ("x", "y", "z")
MESH = pl.DeviceIdType.MESH


def position():
    t, h = lax.axis_index("tm"), lax.axis_index("height")
    return {"x": h % 4, "y": t // 2, "z": h // 4, "k": t % 2}


def device(at):
    return at["y"] * 2 + at["k"], at["z"] * 4 + at["x"]


def moved(at, **by):
    return {n: (v + by.get(n, 0)) % (2 if n == "k" else 4) for n, v in at.items()}


def greet(peers):
    barrier = pltpu.get_barrier_semaphore()
    for peer in peers:
        pl.semaphore_signal(barrier, inc=1, device_id=peer, device_id_type=MESH)
    pl.semaphore_wait(barrier, len(peers))


def spread_kernel(
    kv_ref,
    table_ref,
    window_ref,
    rows0_ref,
    rows1_ref,
    rows2_ref,
    tables_ref,
    local_sem,
    send_sem,
    window_sem,
    rows_sem,
    table_sem,
):
    me = position()
    t, h = lax.axis_index("tm"), lax.axis_index("height")
    rows_refs = (rows0_ref, rows1_ref, rows2_ref)
    later, earlier = (t, (h + 1) % 16), (t, (h + 15) % 16)
    after, before = ((t + 1) % 8, h), ((t + 7) % 8, h)
    peers = [later, earlier, after, before]
    peers += [device(moved(me, **{a: d})) for a in AXES for d in (1, 2, 3)]
    peers += [device(moved(me, k=1))]
    greet(peers)
    sent = []

    def send(src, dst, sem, to):
        copy = pltpu.make_async_remote_copy(
            src_ref=src,
            dst_ref=dst,
            send_sem=send_sem.at[len(sent)],
            recv_sem=sem,
            device_id=to,
            device_id_type=MESH,
        )
        copy.start()
        sent.append(copy)
        return copy

    own_table = tables_ref.at[me["k"], me["z"], me["y"], me["x"]]
    copies = [pltpu.make_async_copy(table_ref, own_table, local_sem.at[0])]
    for part in range(3):
        for n, (kind, low, high, at) in enumerate(PIECES[part]):
            copies.append(
                pltpu.make_async_copy(
                    kv_ref.at[:, kind, low:high],
                    rows_refs[part].at[me[AXES[part]], :, at : at + high - low],
                    local_sem.at[1 + part * 2 + n],
                )
            )
    for copy in copies:
        copy.start()

    def tables(stage, src, dst):
        axis = "xyzk"[stage]
        return [
            send(src, dst, table_sem.at[stage, d - 1], device(moved(me, **{axis: d})))
            for d in range(1, 2 if axis == "k" else 4)
        ]

    table_x = tables(0, table_ref, own_table)
    from_earlier = send(kv_ref, window_ref.at[1, 0], window_sem.at[0], later)
    from_later = send(kv_ref, window_ref.at[1, 2], window_sem.at[1], earlier)
    windows = [
        send(kv_ref, window_ref.at[0, 1], window_sem.at[2], after),
        send(kv_ref, window_ref.at[2, 1], window_sem.at[3], before),
    ]
    near = []
    for part in range(3):
        for way, d in enumerate((1, 3)):
            group = []
            for n, (kind, low, high, at) in enumerate(PIECES[part]):
                group.append(
                    send(
                        kv_ref.at[:, kind, low:high],
                        rows_refs[part].at[me[AXES[part]], :, at : at + high - low],
                        rows_sem.at[part, way, n],
                        device(moved(me, **{AXES[part]: d})),
                    )
                )
            near.append(group)
    copies[0].wait()
    for copy in table_x:
        copy.wait_recv()
    row = tables_ref.at[me["k"], me["z"], me["y"]]
    table_y = tables(1, row, row)
    for copy in table_y:
        copy.wait_recv()
    plane = tables_ref.at[me["k"], me["z"]]
    table_z = tables(2, plane, plane)
    for copy in table_z:
        copy.wait_recv()
    core = tables_ref.at[me["k"]]
    table_k = tables(3, core, core)
    far = []
    for part in (2, 1, 0):
        for way, d in enumerate((1, 3)):
            for copy in near[part * 2 + way]:
                copy.wait_recv()
            block = rows_refs[part].at[moved(me, **{AXES[part]: 4 - d})[AXES[part]], way]
            far.append(
                send(
                    block,
                    block,
                    rows_sem.at[part, 2 + way, 0],
                    device(moved(me, **{AXES[part]: d})),
                )
            )
    for j, copy in ((0, from_earlier), (2, from_later)):
        copy.wait_recv()
        block = window_ref.at[1, j]
        windows.append(send(block, window_ref.at[0, j], window_sem.at[4 + j], after))
        windows.append(send(block, window_ref.at[2, j], window_sem.at[5 + j], before))
    for copy in table_k + far + windows:
        copy.wait_recv()
    for copy in copies[1:]:
        copy.wait()
    for copy in sent:
        copy.wait_send()


def spread(kv, table):
    width = kv.shape[-1]
    hbm = pl.BlockSpec(memory_space=pl.ANY)
    vmem = pl.BlockSpec(memory_space=pltpu.VMEM)
    rows = [jax.ShapeDtypeStruct((4, NW, r, width), kv.dtype) for r in PART_ROWS]
    return pl.pallas_call(
        spread_kernel,
        name="spread",
        out_shape=(
            jax.ShapeDtypeStruct((3, 3) + kv.shape, kv.dtype),
            *rows,
            jax.ShapeDtypeStruct((2, 4, 4, 4) + table.shape, table.dtype),
        ),
        in_specs=[vmem, vmem],
        out_specs=(hbm,) * 5,
        scratch_shapes=[
            pltpu.SemaphoreType.DMA((7,)),
            pltpu.SemaphoreType.DMA((40,)),
            pltpu.SemaphoreType.DMA((8,)),
            pltpu.SemaphoreType.DMA((3, 4, 2)),
            pltpu.SemaphoreType.DMA((4, 3)),
        ],
        compiler_params=pltpu.CompilerParams(collective_id=0, has_side_effects=True),
    )(kv, table)


def pick_kernel(code0, code1, code2, rows0, rows1, rows2, out0, out1, out2):
    step = pl.program_id(0) * 4 + pl.program_id(1)
    tiles = 32

    def one(i, carry):
        for code_ref, rows, out in ((code0, rows0, out0), (code1, rows1, out1), (code2, rows2, out2)):
            code = code_ref[step * tiles + i]
            lane = pl.multiple_of((code & 31) * HEAD_DIM, HEAD_DIM)
            out[0, 0, i] = rows[(i >> 2) & 3, code >> 5, :, pl.ds(lane, HEAD_DIM)]
        return carry

    lax.fori_loop(0, tiles, one, 0, unroll=8)


def pick(codes, rows):
    shapes = [(4, 4, 32, r, HEAD_DIM) for r in PART_ROWS]
    return pl.pallas_call(
        pick_kernel,
        name="pick_tiles",
        out_shape=[jax.ShapeDtypeStruct(s, rows[0].dtype) for s in shapes],
        grid_spec=pltpu.PrefetchScalarGridSpec(
            num_scalar_prefetch=3,
            grid=(4, 4),
            in_specs=[
                pl.BlockSpec(r.shape, lambda i, j, *c: (0, 0, 0, 0), pipeline_mode=pl.Buffered(1))
                for r in rows
            ],
            out_specs=[
                pl.BlockSpec((1, 1) + s[2:], lambda i, j, *c: (i, j, 0, 0, 0)) for s in shapes
            ],
        ),
    )(*codes, *rows)


def exchange_kernel(*refs):
    picked, got, between = refs[:3], refs[3:6], refs[6:9]
    local_sem, send_sem, mid_sem, last_sem = refs[9:]
    me = position()
    routes = [("x", "y", "z"), ("y", "z", "x"), ("z", "x", "y")]
    peers = []
    for axis in AXES:
        for d in (1, 2, 3):
            for k in (0, 1):
                peers.append(device(moved(me, **{axis: d}, k=k)))
    peers.append(device(moved(me, k=1)))
    greet(peers)
    middle = []
    for part in range(3):
        second = routes[part][1]
        group = []
        for n, d in enumerate((1, 3, 2)):
            to = moved(me, **{second: d})
            copy = pltpu.make_async_remote_copy(
                src_ref=picked[part].at[to[second]],
                dst_ref=between[part].at[me[second]],
                send_sem=send_sem.at[part, 0],
                recv_sem=mid_sem.at[part, n],
                device_id=device(to),
                device_id_type=MESH,
            )
            copy.start()
            group.append(copy)
        middle.append(group)
    for n, d in enumerate((0, 3, 1, 2)):
        for part in range(3):
            _, second, third = routes[part]
            came = moved(me, **{second: d})[second]
            if n > 0:
                middle[part][n - 1].wait_recv()
                held = between[part].at[came]
            else:
                held = picked[part].at[came]
            for e in (1, 3, 2, 0):
                for k in (0, 1):
                    to = moved(me, **{third: e}, k=k)
                    src = held.at[to[third], pl.ds(to["k"] * 16, 16)]
                    dst = got[part].at[came, me[third], me["k"]]
                    if e == 0 and k == 0:
                        pltpu.make_async_copy(src, dst, local_sem.at[part]).start()
                    else:
                        pltpu.make_async_remote_copy(
                            src_ref=src,
                            dst_ref=dst,
                            send_sem=send_sem.at[part, 1],
                            recv_sem=last_sem.at[part],
                            device_id=device(to),
                            device_id_type=MESH,
                        ).start()
    for part in range(3):
        whole = got[part].at[:, :, :, 0:14]
        pltpu.make_async_copy(whole, whole, last_sem.at[part]).wait()
        pltpu.make_async_copy(whole, whole, send_sem.at[part, 1]).wait()
        some = got[part].at[:, 0, 0]
        pltpu.make_async_copy(some, some, local_sem.at[part]).wait()
        some = between[part].at[0:3]
        pltpu.make_async_copy(some, some, send_sem.at[part, 0]).wait()


def exchange(picked):
    hbm = pl.BlockSpec(memory_space=pl.ANY)
    got = [jax.ShapeDtypeStruct((4, 4, 2, 16, r, HEAD_DIM), picked[0].dtype) for r in PART_ROWS]
    between = [jax.ShapeDtypeStruct(p.shape, p.dtype) for p in picked]
    outs = pl.pallas_call(
        exchange_kernel,
        name="exchange",
        out_shape=got + between,
        in_specs=[hbm] * 3,
        out_specs=[hbm] * 6,
        scratch_shapes=[
            pltpu.SemaphoreType.DMA((3,)),
            pltpu.SemaphoreType.DMA((3, 2)),
            pltpu.SemaphoreType.DMA((3, 3)),
            pltpu.SemaphoreType.DMA((3,)),
        ],
        compiler_params=pltpu.CompilerParams(collective_id=1, has_side_effects=True),
    )(*picked)
    return [g.reshape(SLOTS, r, HEAD_DIM) for g, r in zip(outs[:3], PART_ROWS)]


def asked_codes(tables):
    at = position()
    t = tables.reshape(2, 4, 4, 4, 8, 4, 2, 4, 4)[:, :, :, :, :4]
    t = lax.dynamic_index_in_dim(t, at["k"], 6, keepdims=False)

    def take(value, which):
        for axis, name in which:
            value = lax.dynamic_index_in_dim(value, at[name], axis, keepdims=True)
        return value

    part0 = take(t, ((3, "x"), (5, "y"), (6, "z")))[:, :, :, 0, :, 0, 0, :]
    part1 = take(t, ((2, "y"), (6, "z"), (7, "x")))[:, :, 0, :, :, :, 0, 0]
    part2 = take(t, ((1, "z"), (5, "y"), (7, "x")))[:, 0, :, :, :, 0, :, 0]
    return [
        jnp.transpose(part0, (2, 1, 0, 4, 3)).reshape(SLOTS),
        jnp.transpose(part1, (1, 2, 0, 4, 3)).reshape(SLOTS),
        jnp.transpose(part2, (2, 1, 0, 4, 3)).reshape(SLOTS),
    ]


def window_kernel(valid_ref, q_ref, *refs):
    own_ref, window_ref, acc_ref, stat_ref = refs

    def block(j, kind, lanes):
        if j == 4:
            return own_ref[:, kind, :, lanes].reshape(ROWS, HEAD_DIM)
        return window_ref[j // 3, j % 3, :, kind, :, lanes].reshape(ROWS, HEAD_DIM)

    for p in range(PAIR):
        lanes = slice(p * HEAD_DIM, (p + 1) * HEAD_DIM)
        query = q_ref[:, lanes]
        parts = []
        for j in range(9):
            keys = block(j, 0, lanes)
            score = lax.dot_general(
                query, keys, (((1,), (1,)), ((), ())), preferred_element_type=jnp.float32
            )
            parts.append(jnp.where(valid_ref[j] > 0, score, NEG))
        scores = jnp.concatenate(parts, axis=-1)
        largest = jnp.max(scores, axis=-1, keepdims=True)
        lifted = jnp.exp2((scores - largest) * EXP2_SCALE)
        total = jnp.sum(lifted, axis=-1, keepdims=True)
        values = jnp.concatenate(
            [block(j, 1, lanes) for j in range(9)], axis=0
        )
        acc_ref[p] = jnp.dot(
            lifted.astype(jnp.bfloat16), values, preferred_element_type=jnp.float32
        )
        lane = lax.broadcasted_iota(jnp.int32, (ROWS, HEAD_DIM), 1)
        stat_ref[p] = jnp.where(lane < HEAD_DIM // 2, largest, total)


def window_attention(valid, queries, kv, window):
    steps = HEADS // PAIR
    width = PAIR * HEAD_DIM
    stat = jax.ShapeDtypeStruct((HEADS, ROWS, HEAD_DIM), jnp.float32)
    block = pl.BlockSpec((NW, 2, CUBE, width), lambda i, v: (0, 0, 0, i))
    out = pl.BlockSpec((PAIR, ROWS, HEAD_DIM), lambda i, v: (i, 0, 0))
    return pl.pallas_call(
        window_kernel,
        name="window_attention",
        out_shape=(stat, stat),
        grid_spec=pltpu.PrefetchScalarGridSpec(
            num_scalar_prefetch=1,
            grid=(steps,),
            in_specs=[
                pl.BlockSpec((ROWS, width), lambda i, v: (0, i)),
                block,
                pl.BlockSpec((3, 3, NW, 2, CUBE, width), lambda i, v: (0, 0, 0, 0, 0, i)),
            ],
            out_specs=(out, out),
        ),
        cost_estimate=pl.CostEstimate(
            flops=HEADS * 4 * ROWS * 9 * ROWS * HEAD_DIM,
            bytes_accessed=20_000_000,
            transcendentals=HEADS * ROWS * 9 * ROWS,
        ),
    )(valid, queries, kv, window)


def far_kernel(
    slot_ref, q_ref, tiles0, tiles1, tiles2, acc_ref, stat_ref, w_ref, out_ref, total
):
    step = pl.program_id(0)
    steps = pl.num_programs(0)

    @pl.when(step == 0)
    def _():
        total[...] = jnp.zeros_like(total)

    heads = []
    for p in range(PAIR):
        cubes = []
        for c in range(NW):
            rows = slice(c * CUBE, (c + 1) * CUBE)
            query = q_ref[rows, p * HEAD_DIM : (p + 1) * HEAD_DIM]
            keys, values = [], []
            for f in range(FAR):
                slot = slot_ref[(c * HEADS + step * PAIR + p) * FAR + f]
                in0, in1, in2 = slot & (SLOTS - 1), (slot >> 9) & (SLOTS - 1), slot >> 18
                keys += [tiles0[in0], tiles1[in1, 0:16]]
                values += [tiles1[in1, 16:48], tiles2[in2]]
            keys = jnp.concatenate(keys, axis=0)
            values = jnp.concatenate(values, axis=0)
            scores = lax.dot_general(
                query, keys, (((1,), (1,)), ((), ())), preferred_element_type=jnp.float32
            )
            near_max = stat_ref[p, rows, 0:1]
            near_sum = stat_ref[p, rows, HEAD_DIM // 2 : HEAD_DIM // 2 + 1]
            largest = jnp.maximum(near_max, jnp.max(scores, axis=-1, keepdims=True))
            lifted = jnp.exp2((scores - largest) * EXP2_SCALE)
            fade = jnp.exp2((near_max - largest) * EXP2_SCALE)
            weight = near_sum * fade + jnp.sum(lifted, axis=-1, keepdims=True)
            summed = acc_ref[p, rows] * fade + jnp.dot(
                lifted.astype(jnp.bfloat16), values, preferred_element_type=jnp.float32
            )
            cubes.append((summed / weight).astype(jnp.bfloat16))
        heads.append(jnp.concatenate(cubes, axis=0))
    attended = jnp.concatenate(heads, axis=1)
    total[...] += jnp.dot(attended, w_ref[...], preferred_element_type=jnp.float32)

    @pl.when(step == steps - 1)
    def _():
        out_ref[...] = total[...].astype(out_ref.dtype)


def far_attention(far_slot, queries, tiles, acc, stat, out_weight):
    steps = HEADS // PAIR
    width = PAIR * HEAD_DIM
    model = queries.shape[1]
    near = pl.BlockSpec((PAIR, ROWS, HEAD_DIM), lambda i, s: (i, 0, 0))
    return pl.pallas_call(
        far_kernel,
        name="far_attention",
        out_shape=jax.ShapeDtypeStruct((ROWS, model), queries.dtype),
        grid_spec=pltpu.PrefetchScalarGridSpec(
            num_scalar_prefetch=1,
            grid=(steps,),
            in_specs=[
                pl.BlockSpec((ROWS, width), lambda i, s: (0, i)),
                *[
                    pl.BlockSpec(x.shape, lambda i, s: (0, 0, 0), pipeline_mode=pl.Buffered(1))
                    for x in tiles
                ],
                near,
                near,
                pl.BlockSpec((width, model), lambda i, s: (i, 0)),
            ],
            out_specs=pl.BlockSpec((ROWS, model), lambda i, s: (0, 0)),
            scratch_shapes=[pltpu.VMEM((ROWS, model), jnp.float32)],
        ),
        cost_estimate=pl.CostEstimate(
            flops=HEADS * 4 * ROWS * FAR * CUBE * HEAD_DIM + 2 * ROWS * model * model,
            bytes_accessed=50_000_000,
            transcendentals=HEADS * ROWS * FAR * CUBE,
        ),
    )(far_slot, queries, *tiles, acc, stat, out_weight)


def body(queries, keys_values, far_cubes, out_weight):
    tm_count = lax.axis_size("tm")
    height_count = lax.axis_size("height")
    device_count = tm_count * height_count
    model = queries.shape[-1]
    far = far_cubes.reshape(NW, HEADS, FAR)
    requests, far_slot = request_tables(far, device_count)
    kv = keys_values.reshape(NW, 2, CUBE, model)
    window, *rows, tables = spread(kv, requests)
    tiles = exchange(pick(asked_codes(tables), rows))
    offsets = jnp.arange(3, dtype=jnp.int32) - 1
    times = lax.axis_index("tm") + offsets
    heights = lax.axis_index("height") + offsets
    valid = ((times >= 0) & (times < tm_count))[:, None]
    valid = valid & ((heights >= 0) & (heights < height_count))[None, :]
    valid = valid.reshape(9).astype(jnp.int32)
    flat_queries = queries.reshape(ROWS, model)
    acc, stat = window_attention(valid, flat_queries, kv, window)
    output = far_attention(
        far_slot.reshape(NW * HEADS * FAR), flat_queries, tiles, acc, stat, out_weight
    )
    return output.reshape(queries.shape)


def solution(mesh):
    in_specs = (
        P("tm", "height", None, None, None),
        P("tm", "height", None, None, None, None),
        P("tm", "height", None, None, None),
        P(),
    )
    out_specs = P("tm", "height", None, None, None)
    return jax.shard_map(body, mesh=mesh, in_specs=in_specs, out_specs=out_specs, check_vma=False)
```

```python
import functools
import math

import jax
import jax.numpy as jnp
from jax import lax
from jax.experimental import pallas as pl
from jax.experimental.pallas import tpu as pltpu
from jax.sharding import PartitionSpec as P

HEADS = 24
HEAD_DIM = 128
CUBE = 64
FAR = 16
NW = 2
SLOTS = 512
PAIR = 2
ROWS = NW * CUBE
NEG = -1e30
EXP2_SCALE = math.log2(math.e) / math.sqrt(HEAD_DIM)


def request_tables(far, device_count):
    capacity = SLOTS // device_count
    cubes = device_count * NW
    hit = far[:, :, :, None] == jnp.arange(cubes, dtype=jnp.int32)
    wanted = jnp.any(hit, axis=(0, 2))
    wanted = jnp.transpose(wanted.reshape(HEADS, device_count, NW), (1, 2, 0))
    wanted = wanted.reshape(device_count, NW * HEADS)
    codes = jnp.arange(NW * HEADS, dtype=jnp.int32)
    before = (codes[:, None] < codes[None, :]).astype(jnp.bfloat16)
    rank = jnp.dot(wanted.astype(jnp.bfloat16), before, preferred_element_type=jnp.float32)
    rank = rank.astype(jnp.int32)
    chosen = wanted[:, :, None] & (rank[:, :, None] == jnp.arange(2 * capacity, dtype=jnp.int32))
    labels = codes // HEADS * 32 + codes % HEADS
    requests = jnp.sum(jnp.where(chosen, labels[None, :, None], 0), axis=1)
    slot = rank + jnp.arange(device_count, dtype=jnp.int32)[:, None] * capacity
    slot = jnp.transpose(slot.reshape(device_count, NW, HEADS), (2, 0, 1)).reshape(HEADS, cubes)
    far_slot = jnp.sum(jnp.where(hit, slot[None, :, None, :], 0), axis=-1)
    rank, owner = far_slot % capacity, far_slot // capacity
    y, k, z, x = owner // 32, owner // 16 % 2, owner // 4 % 4, owner % 4
    in_x = (((y * 4 + z) * 2 + k) * 4 + x) * capacity + rank
    in_y = (((z * 4 + x) * 2 + k) * 4 + y) * capacity + rank
    in_z = (((x * 4 + y) * 2 + k) * 4 + z) * capacity + rank
    return requests.T, in_x + in_y * SLOTS + in_z * SLOTS * SLOTS


PART_ROWS = (48, 48, 32)
PIECES = (
    ((0, 0, 48, 0),),
    ((0, 48, 64, 0), (1, 0, 32, 16)),
    ((1, 32, 64, 0),),
)
AXES = ("x", "y", "z")
MESH = pl.DeviceIdType.MESH


def position():
    t, h = lax.axis_index("tm"), lax.axis_index("height")
    return {"x": h % 4, "y": t // 2, "z": h // 4, "k": t % 2}


def device(at):
    return at["y"] * 2 + at["k"], at["z"] * 4 + at["x"]


def moved(at, **by):
    return {n: (v + by.get(n, 0)) % (2 if n == "k" else 4) for n, v in at.items()}


def greet(peers):
    barrier = pltpu.get_barrier_semaphore()
    for peer in peers:
        pl.semaphore_signal(barrier, inc=1, device_id=peer, device_id_type=MESH)
    pl.semaphore_wait(barrier, len(peers))


def spread_kernel(
    kv_ref,
    table_ref,
    rows0_ref,
    rows1_ref,
    rows2_ref,
    tables_ref,
    local_sem,
    send_sem,
    rows_sem,
    table_sem,
):
    me = position()
    rows_refs = (rows0_ref, rows1_ref, rows2_ref)
    peers = [device(moved(me, **{a: d})) for a in AXES for d in (1, 2, 3)]
    peers += [device(moved(me, k=1))]
    greet(peers)
    sent = []

    def send(src, dst, sem, to):
        copy = pltpu.make_async_remote_copy(
            src_ref=src,
            dst_ref=dst,
            send_sem=send_sem.at[len(sent)],
            recv_sem=sem,
            device_id=to,
            device_id_type=MESH,
        )
        copy.start()
        sent.append(copy)
        return copy

    own_table = tables_ref.at[me["k"], me["z"], me["y"], me["x"]]
    copies = [pltpu.make_async_copy(table_ref, own_table, local_sem.at[0])]
    for part in range(3):
        for n, (kind, low, high, at) in enumerate(PIECES[part]):
            copies.append(
                pltpu.make_async_copy(
                    kv_ref.at[:, kind, low:high],
                    rows_refs[part].at[me[AXES[part]], :, at : at + high - low],
                    local_sem.at[1 + part * 2 + n],
                )
            )
    for copy in copies:
        copy.start()

    def tables(stage, src, dst):
        axis = "xyzk"[stage]
        return [
            send(src, dst, table_sem.at[stage, d - 1], device(moved(me, **{axis: d})))
            for d in range(1, 2 if axis == "k" else 4)
        ]

    def nearest(part):
        groups = []
        for way, d in enumerate((1, 3)):
            group = []
            for n, (kind, low, high, at) in enumerate(PIECES[part]):
                group.append(
                    send(
                        kv_ref.at[:, kind, low:high],
                        rows_refs[part].at[me[AXES[part]], :, at : at + high - low],
                        rows_sem.at[part, way, n],
                        device(moved(me, **{AXES[part]: d})),
                    )
                )
            groups.append(group)
        return groups

    table_x = tables(0, table_ref, own_table)
    near = [nearest(0)]
    copies[0].wait()
    for copy in table_x:
        copy.wait_recv()
    row = tables_ref.at[me["k"], me["z"], me["y"]]
    table_y = tables(1, row, row)
    near.append(nearest(1))
    for copy in table_y:
        copy.wait_recv()
    plane = tables_ref.at[me["k"], me["z"]]
    table_z = tables(2, plane, plane)
    near.append(nearest(2))
    for copy in table_z:
        copy.wait_recv()
    core = tables_ref.at[me["k"]]
    table_k = tables(3, core, core)
    far = []
    for part in (0, 1, 2):
        for way, d in enumerate((1, 3)):
            for copy in near[part][way]:
                copy.wait_recv()
            block = rows_refs[part].at[moved(me, **{AXES[part]: 4 - d})[AXES[part]], way]
            far.append(
                send(
                    block,
                    block,
                    rows_sem.at[part, 2 + way, 0],
                    device(moved(me, **{AXES[part]: d})),
                )
            )
    for copy in table_k + far:
        copy.wait_recv()
    for copy in copies[1:]:
        copy.wait()
    for copy in sent:
        copy.wait_send()


def spread(kv, table):
    width = kv.shape[-1]
    hbm = pl.BlockSpec(memory_space=pl.ANY)
    vmem = pl.BlockSpec(memory_space=pltpu.VMEM)
    rows = [jax.ShapeDtypeStruct((4, NW, r, width), kv.dtype) for r in PART_ROWS]
    return pl.pallas_call(
        spread_kernel,
        name="spread",
        out_shape=(
            *rows,
            jax.ShapeDtypeStruct((2, 4, 4, 4) + table.shape, table.dtype),
        ),
        in_specs=[vmem, vmem],
        out_specs=(hbm,) * 4,
        scratch_shapes=[
            pltpu.SemaphoreType.DMA((7,)),
            pltpu.SemaphoreType.DMA((32,)),
            pltpu.SemaphoreType.DMA((3, 4, 2)),
            pltpu.SemaphoreType.DMA((4, 3)),
        ],
        compiler_params=pltpu.CompilerParams(collective_id=0, has_side_effects=True),
    )(kv, table)


def pick_kernel(code0, code1, code2, rows0, rows1, rows2, out0, out1, out2):
    step = pl.program_id(0) * 4 + pl.program_id(1)
    tiles = 32

    def one(i, carry):
        for code_ref, rows, out in ((code0, rows0, out0), (code1, rows1, out1), (code2, rows2, out2)):
            code = code_ref[step * tiles + i]
            lane = pl.multiple_of((code & 31) * HEAD_DIM, HEAD_DIM)
            out[0, 0, i] = rows[(i >> 2) & 3, code >> 5, :, pl.ds(lane, HEAD_DIM)]
        return carry

    lax.fori_loop(0, tiles, one, 0, unroll=8)


def pick(codes, rows):
    shapes = [(4, 4, 32, r, HEAD_DIM) for r in PART_ROWS]
    return pl.pallas_call(
        pick_kernel,
        name="pick_tiles",
        out_shape=[jax.ShapeDtypeStruct(s, rows[0].dtype) for s in shapes],
        grid_spec=pltpu.PrefetchScalarGridSpec(
            num_scalar_prefetch=3,
            grid=(4, 4),
            in_specs=[
                pl.BlockSpec(r.shape, lambda i, j, *c: (0, 0, 0, 0), pipeline_mode=pl.Buffered(1))
                for r in rows
            ],
            out_specs=[
                pl.BlockSpec((1, 1) + s[2:], lambda i, j, *c: (i, j, 0, 0, 0)) for s in shapes
            ],
        ),
    )(*codes, *rows)


def window_heads(i, valid, q_ref, own_ref, window_ref, acc_ref, stat_ref):
    def block(j, kind, lanes):
        ref = own_ref if j == 4 else window_ref.at[j // 3, j % 3]
        return ref[:, kind, :, lanes].reshape(ROWS, HEAD_DIM)

    for p in range(PAIR):
        head = i * PAIR + p
        lanes = pl.ds(pl.multiple_of(head * HEAD_DIM, HEAD_DIM), HEAD_DIM)
        query = q_ref[:, lanes]
        parts = []
        for j in range(9):
            keys = block(j, 0, lanes)
            score = lax.dot_general(
                query, keys, (((1,), (1,)), ((), ())), preferred_element_type=jnp.float32
            )
            parts.append(jnp.where(valid[j] > 0, score, NEG))
        scores = jnp.concatenate(parts, axis=-1)
        largest = jnp.max(scores, axis=-1, keepdims=True)
        lifted = jnp.exp2((scores - largest) * EXP2_SCALE)
        total = jnp.sum(lifted, axis=-1, keepdims=True)
        values = jnp.concatenate([block(j, 1, lanes) for j in range(9)], axis=0)
        acc_ref[head] = jnp.dot(
            lifted.astype(jnp.bfloat16), values, preferred_element_type=jnp.float32
        )
        lane = lax.broadcasted_iota(jnp.int32, (ROWS, HEAD_DIM), 1)
        stat_ref[head] = jnp.where(lane < HEAD_DIM // 2, largest, total)


def exchange_kernel(*refs):
    picked, (kv_ref, q_ref), got, between = refs[:3], refs[3:5], refs[5:8], refs[8:11]
    acc_ref, stat_ref, window_ref = refs[11:14]
    local_sem, send_sem, mid_sem, last_sem, halo_send_sem, halo_sem = refs[14:]
    me = position()
    t, h = lax.axis_index("tm"), lax.axis_index("height")
    t_count, h_count = lax.axis_size("tm"), lax.axis_size("height")
    later, earlier = (t, (h + 1) % h_count), (t, (h + h_count - 1) % h_count)
    after, before = ((t + 1) % t_count, h), ((t + t_count - 1) % t_count, h)
    routes = [("x", "y", "z"), ("y", "z", "x"), ("z", "x", "y")]
    peers = [later, earlier, after, before]
    for axis in AXES:
        for d in (1, 2, 3):
            for k in (0, 1):
                peers.append(device(moved(me, **{axis: d}, k=k)))
    peers.append(device(moved(me, k=1)))
    greet(peers)
    halo = []

    def neighbour(src, a, b, to):
        copy = pltpu.make_async_remote_copy(
            src_ref=src,
            dst_ref=window_ref.at[a, b],
            send_sem=halo_send_sem.at[len(halo)],
            recv_sem=halo_sem.at[len(halo)],
            device_id=to,
            device_id_type=MESH,
        )
        copy.start()
        halo.append(copy)

    neighbour(kv_ref, 1, 0, later)
    neighbour(kv_ref, 1, 2, earlier)
    neighbour(kv_ref, 0, 1, after)
    neighbour(kv_ref, 2, 1, before)
    middle = []
    for part in range(3):
        second = routes[part][1]
        group = []
        for n, d in enumerate((1, 3, 2)):
            to = moved(me, **{second: d})
            copy = pltpu.make_async_remote_copy(
                src_ref=picked[part].at[to[second]],
                dst_ref=between[part].at[me[second]],
                send_sem=send_sem.at[part, 0],
                recv_sem=mid_sem.at[part, n],
                device_id=device(to),
                device_id_type=MESH,
            )
            copy.start()
            group.append(copy)
        middle.append(group)
    for n, d in enumerate((0, 3, 1, 2)):
        if n == 1:
            for came, j in ((0, 0), (1, 2)):
                halo[came].wait_recv()
                neighbour(window_ref.at[1, j], 0, j, after)
                neighbour(window_ref.at[1, j], 2, j, before)
        for part in range(3):
            _, second, third = routes[part]
            came = moved(me, **{second: d})[second]
            if n > 0:
                middle[part][n - 1].wait_recv()
                held = between[part].at[came]
            else:
                held = picked[part].at[came]
            for e in (1, 3, 2, 0):
                for k in (0, 1):
                    to = moved(me, **{third: e}, k=k)
                    src = held.at[to[third], pl.ds(to["k"] * 16, 16)]
                    dst = got[part].at[came, me[third], me["k"]]
                    if e == 0 and k == 0:
                        pltpu.make_async_copy(src, dst, local_sem.at[part]).start()
                    else:
                        pltpu.make_async_remote_copy(
                            src_ref=src,
                            dst_ref=dst,
                            send_sem=send_sem.at[part, 1],
                            recv_sem=last_sem.at[part],
                            device_id=device(to),
                            device_id_type=MESH,
                        ).start()
    for copy in halo[2:]:
        copy.wait_recv()
    valid = []
    for a in (-1, 0, 1):
        for b in (-1, 0, 1):
            inside = (t + a >= 0) & (t + a < t_count) & (h + b >= 0) & (h + b < h_count)
            valid.append(inside.astype(jnp.int32))

    @pl.loop(0, HEADS // PAIR)
    def _(i):
        window_heads(i, valid, q_ref, kv_ref, window_ref, acc_ref, stat_ref)

    for copy in halo:
        copy.wait_send()
    for part in range(3):
        whole = got[part].at[:, :, :, 0:14]
        pltpu.make_async_copy(whole, whole, last_sem.at[part]).wait()
        pltpu.make_async_copy(whole, whole, send_sem.at[part, 1]).wait()
        some = got[part].at[:, 0, 0]
        pltpu.make_async_copy(some, some, local_sem.at[part]).wait()
        some = between[part].at[0:3]
        pltpu.make_async_copy(some, some, send_sem.at[part, 0]).wait()


def exchange(picked, kv, queries):
    hbm = pl.BlockSpec(memory_space=pl.ANY)
    vmem = pl.BlockSpec(memory_space=pltpu.VMEM)
    got = [jax.ShapeDtypeStruct((4, 4, 2, 16, r, HEAD_DIM), picked[0].dtype) for r in PART_ROWS]
    between = [jax.ShapeDtypeStruct(p.shape, p.dtype) for p in picked]
    stat = jax.ShapeDtypeStruct((HEADS, ROWS, HEAD_DIM), jnp.float32)
    outs = pl.pallas_call(
        exchange_kernel,
        name="exchange",
        out_shape=got + between + [stat, stat],
        in_specs=[hbm] * 3 + [vmem] * 2,
        out_specs=[hbm] * 6 + [vmem] * 2,
        scratch_shapes=[
            pltpu.VMEM((3, 3) + kv.shape, kv.dtype),
            pltpu.SemaphoreType.DMA((3,)),
            pltpu.SemaphoreType.DMA((3, 2)),
            pltpu.SemaphoreType.DMA((3, 3)),
            pltpu.SemaphoreType.DMA((3,)),
            pltpu.SemaphoreType.DMA((8,)),
            pltpu.SemaphoreType.DMA((8,)),
        ],
        compiler_params=pltpu.CompilerParams(collective_id=1, has_side_effects=True),
    )(*picked, kv, queries)
    tiles = [g.reshape(SLOTS, r, HEAD_DIM) for g, r in zip(outs[:3], PART_ROWS)]
    return tiles, outs[6], outs[7]


def asked_codes(tables):
    at = position()
    t = tables.reshape(2, 4, 4, 4, 8, 4, 2, 4, 4)[:, :, :, :, :4]
    t = lax.dynamic_index_in_dim(t, at["k"], 6, keepdims=False)

    def take(value, which):
        for axis, name in which:
            value = lax.dynamic_index_in_dim(value, at[name], axis, keepdims=True)
        return value

    part0 = take(t, ((3, "x"), (5, "y"), (6, "z")))[:, :, :, 0, :, 0, 0, :]
    part1 = take(t, ((2, "y"), (6, "z"), (7, "x")))[:, :, 0, :, :, :, 0, 0]
    part2 = take(t, ((1, "z"), (5, "y"), (7, "x")))[:, 0, :, :, :, 0, :, 0]
    return [
        jnp.transpose(part0, (2, 1, 0, 4, 3)).reshape(SLOTS),
        jnp.transpose(part1, (1, 2, 0, 4, 3)).reshape(SLOTS),
        jnp.transpose(part2, (2, 1, 0, 4, 3)).reshape(SLOTS),
    ]


def far_kernel(
    slot_ref, q_ref, tiles0, tiles1, tiles2, acc_ref, stat_ref, w_ref, out_ref, total
):
    step = pl.program_id(0)
    steps = pl.num_programs(0)

    @pl.when(step == 0)
    def _():
        total[...] = jnp.zeros_like(total)

    heads = []
    for p in range(PAIR):
        cubes = []
        for c in range(NW):
            rows = slice(c * CUBE, (c + 1) * CUBE)
            query = q_ref[rows, p * HEAD_DIM : (p + 1) * HEAD_DIM]
            keys, values = [], []
            for f in range(FAR):
                slot = slot_ref[(c * HEADS + step * PAIR + p) * FAR + f]
                in0, in1, in2 = slot & (SLOTS - 1), (slot >> 9) & (SLOTS - 1), slot >> 18
                keys += [tiles0[in0], tiles1[in1, 0:16]]
                values += [tiles1[in1, 16:48], tiles2[in2]]
            keys = jnp.concatenate(keys, axis=0)
            values = jnp.concatenate(values, axis=0)
            scores = lax.dot_general(
                query, keys, (((1,), (1,)), ((), ())), preferred_element_type=jnp.float32
            )
            near_max = stat_ref[p, rows, 0:1]
            near_sum = stat_ref[p, rows, HEAD_DIM // 2 : HEAD_DIM // 2 + 1]
            largest = jnp.maximum(near_max, jnp.max(scores, axis=-1, keepdims=True))
            lifted = jnp.exp2((scores - largest) * EXP2_SCALE)
            fade = jnp.exp2((near_max - largest) * EXP2_SCALE)
            weight = near_sum * fade + jnp.sum(lifted, axis=-1, keepdims=True)
            summed = acc_ref[p, rows] * fade + jnp.dot(
                lifted.astype(jnp.bfloat16), values, preferred_element_type=jnp.float32
            )
            cubes.append((summed / weight).astype(jnp.bfloat16))
        heads.append(jnp.concatenate(cubes, axis=0))
    attended = jnp.concatenate(heads, axis=1)
    total[...] += jnp.dot(attended, w_ref[...], preferred_element_type=jnp.float32)

    @pl.when(step == steps - 1)
    def _():
        out_ref[...] = total[...].astype(out_ref.dtype)


def far_attention(far_slot, queries, tiles, acc, stat, out_weight):
    steps = HEADS // PAIR
    width = PAIR * HEAD_DIM
    model = queries.shape[1]
    near = pl.BlockSpec((PAIR, ROWS, HEAD_DIM), lambda i, s: (i, 0, 0))
    return pl.pallas_call(
        far_kernel,
        name="far_attention",
        out_shape=jax.ShapeDtypeStruct((ROWS, model), queries.dtype),
        grid_spec=pltpu.PrefetchScalarGridSpec(
            num_scalar_prefetch=1,
            grid=(steps,),
            in_specs=[
                pl.BlockSpec((ROWS, width), lambda i, s: (0, i)),
                *[
                    pl.BlockSpec(x.shape, lambda i, s: (0, 0, 0), pipeline_mode=pl.Buffered(1))
                    for x in tiles
                ],
                near,
                near,
                pl.BlockSpec((width, model), lambda i, s: (i, 0)),
            ],
            out_specs=pl.BlockSpec((ROWS, model), lambda i, s: (0, 0)),
            scratch_shapes=[pltpu.VMEM((ROWS, model), jnp.float32)],
        ),
        cost_estimate=pl.CostEstimate(
            flops=HEADS * 4 * ROWS * FAR * CUBE * HEAD_DIM + 2 * ROWS * model * model,
            bytes_accessed=50_000_000,
            transcendentals=HEADS * ROWS * FAR * CUBE,
        ),
    )(far_slot, queries, *tiles, acc, stat, out_weight)


def body(queries, keys_values, far_cubes, out_weight):
    tm_count = lax.axis_size("tm")
    height_count = lax.axis_size("height")
    device_count = tm_count * height_count
    model = queries.shape[-1]
    far = far_cubes.reshape(NW, HEADS, FAR)
    requests, far_slot = request_tables(far, device_count)
    kv = keys_values.reshape(NW, 2, CUBE, model)
    *rows, tables = spread(kv, requests)
    flat_queries = queries.reshape(ROWS, model)
    tiles, acc, stat = exchange(pick(asked_codes(tables), rows), kv, flat_queries)
    output = far_attention(
        far_slot.reshape(NW * HEADS * FAR), flat_queries, tiles, acc, stat, out_weight
    )
    return output.reshape(queries.shape)


def solution(mesh):
    in_specs = (
        P("tm", "height", None, None, None),
        P("tm", "height", None, None, None, None),
        P("tm", "height", None, None, None),
        P(),
    )
    out_specs = P("tm", "height", None, None, None)
    return jax.shard_map(body, mesh=mesh, in_specs=in_specs, out_specs=out_specs, check_vma=False)
```

```python
import functools
import math

import jax
import jax.numpy as jnp
from jax import lax
from jax.experimental import pallas as pl
from jax.experimental.pallas import tpu as pltpu
from jax.sharding import PartitionSpec as P

HEADS = 24
HEAD_DIM = 128
CUBE = 64
FAR = 16
NW = 2
SLOTS = 512
PAIR = 2
ROWS = NW * CUBE
NEG = -1e30
EXP2_SCALE = math.log2(math.e) / math.sqrt(HEAD_DIM)


def request_tables(far, device_count):
    capacity = SLOTS // device_count
    cubes = device_count * NW
    hit = far[:, :, :, None] == jnp.arange(cubes, dtype=jnp.int32)
    wanted = jnp.any(hit, axis=(0, 2))
    wanted = jnp.transpose(wanted.reshape(HEADS, device_count, NW), (1, 2, 0))
    wanted = wanted.reshape(device_count, NW * HEADS)
    codes = jnp.arange(NW * HEADS, dtype=jnp.int32)
    before = (codes[:, None] < codes[None, :]).astype(jnp.bfloat16)
    rank = jnp.dot(wanted.astype(jnp.bfloat16), before, preferred_element_type=jnp.float32)
    rank = rank.astype(jnp.int32)
    chosen = wanted[:, :, None] & (rank[:, :, None] == jnp.arange(2 * capacity, dtype=jnp.int32))
    requests = jnp.sum(jnp.where(chosen, codes[None, :, None], 0), axis=1)
    slot = rank + jnp.arange(device_count, dtype=jnp.int32)[:, None] * capacity
    slot = jnp.transpose(slot.reshape(device_count, NW, HEADS), (2, 0, 1)).reshape(HEADS, cubes)
    far_slot = jnp.sum(jnp.where(hit, slot[None, :, None, :], 0), axis=-1)
    rank, owner = far_slot % capacity, far_slot // capacity
    y, k, z, x = owner // 32, owner // 16 % 2, owner // 4 % 4, owner % 4
    in_x = (((y * 4 + z) * 2 + k) * 4 + x) * capacity + rank
    in_y = (((z * 4 + x) * 2 + k) * 4 + y) * capacity + rank
    in_z = (((x * 4 + y) * 2 + k) * 4 + z) * capacity + rank
    return requests.T, in_x + in_y * SLOTS + in_z * SLOTS * SLOTS


PART_ROWS = (48, 48, 32)
PIECES = (
    ((0, 0, 48, 0),),
    ((0, 48, 64, 0), (1, 0, 32, 16)),
    ((1, 32, 64, 0),),
)
AXES = ("x", "y", "z")
MESH = pl.DeviceIdType.MESH


def position():
    t, h = lax.axis_index("tm"), lax.axis_index("height")
    return {"x": h % 4, "y": t // 2, "z": h // 4, "k": t % 2}


def device(at):
    return at["y"] * 2 + at["k"], at["z"] * 4 + at["x"]


def moved(at, **by):
    return {n: (v + by.get(n, 0)) % (2 if n == "k" else 4) for n, v in at.items()}


def greet(peers):
    barrier = pltpu.get_barrier_semaphore()
    for peer in peers:
        pl.semaphore_signal(barrier, inc=1, device_id=peer, device_id_type=MESH)
    pl.semaphore_wait(barrier, len(peers))


def spread_kernel(
    kv_ref,
    table_ref,
    rows0_ref,
    rows1_ref,
    rows2_ref,
    tables_ref,
    local_sem,
    send_sem,
    rows_sem,
    table_sem,
):
    me = position()
    rows_refs = (rows0_ref, rows1_ref, rows2_ref)
    peers = [device(moved(me, **{a: d})) for a in AXES for d in (1, 2, 3)]
    peers += [device(moved(me, k=1))]
    greet(peers)
    sent = []

    def send(src, dst, sem, to):
        copy = pltpu.make_async_remote_copy(
            src_ref=src,
            dst_ref=dst,
            send_sem=send_sem.at[len(sent)],
            recv_sem=sem,
            device_id=to,
            device_id_type=MESH,
        )
        copy.start()
        sent.append(copy)
        return copy

    own_table = tables_ref.at[me["k"], me["z"], me["y"], me["x"]]
    copies = [pltpu.make_async_copy(table_ref, own_table, local_sem.at[0])]
    for part in range(3):
        for n, (kind, low, high, at) in enumerate(PIECES[part]):
            copies.append(
                pltpu.make_async_copy(
                    kv_ref.at[:, kind, low:high],
                    rows_refs[part].at[me[AXES[part]], :, at : at + high - low],
                    local_sem.at[1 + part * 2 + n],
                )
            )
    for copy in copies:
        copy.start()

    def tables(stage, src, dst):
        axis = "xyzk"[stage]
        return [
            send(src, dst, table_sem.at[stage, d - 1], device(moved(me, **{axis: d})))
            for d in range(1, 2 if axis == "k" else 4)
        ]

    def nearest(part):
        groups = []
        for way, d in enumerate((1, 3)):
            group = []
            for n, (kind, low, high, at) in enumerate(PIECES[part]):
                group.append(
                    send(
                        kv_ref.at[:, kind, low:high],
                        rows_refs[part].at[me[AXES[part]], :, at : at + high - low],
                        rows_sem.at[part, way, n],
                        device(moved(me, **{AXES[part]: d})),
                    )
                )
            groups.append(group)
        return groups

    table_x = tables(0, table_ref, own_table)
    near = [nearest(0)]
    copies[0].wait()
    for copy in table_x:
        copy.wait_recv()
    row = tables_ref.at[me["k"], me["z"], me["y"]]
    table_y = tables(1, row, row)
    near.append(nearest(1))
    for copy in table_y:
        copy.wait_recv()
    plane = tables_ref.at[me["k"], me["z"]]
    table_z = tables(2, plane, plane)
    near.append(nearest(2))
    for copy in table_z:
        copy.wait_recv()
    core = tables_ref.at[me["k"]]
    table_k = tables(3, core, core)
    far = []
    for part in (0, 1, 2):
        for way, d in enumerate((1, 3)):
            for copy in near[part][way]:
                copy.wait_recv()
            block = rows_refs[part].at[moved(me, **{AXES[part]: 4 - d})[AXES[part]], way]
            far.append(
                send(
                    block,
                    block,
                    rows_sem.at[part, 2 + way, 0],
                    device(moved(me, **{AXES[part]: d})),
                )
            )
    for copy in table_k + far:
        copy.wait_recv()
    for copy in copies[1:]:
        copy.wait()
    for copy in sent:
        copy.wait_send()


def spread(kv, table):
    width = kv.shape[-1]
    hbm = pl.BlockSpec(memory_space=pl.ANY)
    vmem = pl.BlockSpec(memory_space=pltpu.VMEM)
    rows = [jax.ShapeDtypeStruct((4, NW, r, width), kv.dtype) for r in PART_ROWS]
    return pl.pallas_call(
        spread_kernel,
        name="spread",
        out_shape=(
            *rows,
            jax.ShapeDtypeStruct((2, 4, 4, 4) + table.shape, table.dtype),
        ),
        in_specs=[vmem, vmem],
        out_specs=(hbm,) * 4,
        scratch_shapes=[
            pltpu.SemaphoreType.DMA((7,)),
            pltpu.SemaphoreType.DMA((32,)),
            pltpu.SemaphoreType.DMA((3, 4, 2)),
            pltpu.SemaphoreType.DMA((4, 3)),
        ],
        compiler_params=pltpu.CompilerParams(collective_id=0, has_side_effects=True),
    )(kv, table)


def window_heads(i, valid, q_ref, own_ref, window_ref, acc_ref, stat_ref):
    def block(j, kind, lanes):
        ref = own_ref if j == 4 else window_ref.at[j // 3, j % 3]
        return ref[:, kind, :, lanes].reshape(ROWS, HEAD_DIM)

    for p in range(PAIR):
        head = i * PAIR + p
        lanes = pl.ds(pl.multiple_of(head * HEAD_DIM, HEAD_DIM), HEAD_DIM)
        query = q_ref[:, lanes]
        parts = []
        for j in range(9):
            keys = block(j, 0, lanes)
            score = lax.dot_general(
                query, keys, (((1,), (1,)), ((), ())), preferred_element_type=jnp.float32
            )
            parts.append(jnp.where(valid[j] > 0, score, NEG))
        scores = jnp.concatenate(parts, axis=-1)
        largest = jnp.max(scores, axis=-1, keepdims=True)
        lifted = jnp.exp2((scores - largest) * EXP2_SCALE)
        total = jnp.sum(lifted, axis=-1, keepdims=True)
        values = jnp.concatenate([block(j, 1, lanes) for j in range(9)], axis=0)
        acc_ref[head] = jnp.dot(
            lifted.astype(jnp.bfloat16), values, preferred_element_type=jnp.float32
        )
        lane = lax.broadcasted_iota(jnp.int32, (ROWS, HEAD_DIM), 1)
        stat_ref[head] = jnp.where(lane < HEAD_DIM // 2, largest, total)


def exchange_kernel(*refs):
    code_ref, rows_refs, (kv_ref, q_ref) = refs[0], refs[1:4], refs[4:6]
    got, between, picked, (acc_ref, stat_ref) = refs[6:9], refs[9:12], refs[12:15], refs[15:17]
    window_ref, rows, chosen = refs[17], refs[18:21], refs[21:24]
    local_sem, send_sem, mid_sem, last_sem, halo_send_sem, halo_sem, rows_sem, chosen_sem = refs[24:]
    for part in range(3):
        for code in range(NW * HEADS):
            lane = code % HEADS * HEAD_DIM
            pltpu.make_async_copy(
                rows_refs[part].at[:, code // HEADS, :, lane : lane + HEAD_DIM],
                rows[part].at[:, code],
                rows_sem.at[part],
            ).start()
    me = position()
    t, h = lax.axis_index("tm"), lax.axis_index("height")
    t_count, h_count = lax.axis_size("tm"), lax.axis_size("height")
    later, earlier = (t, (h + 1) % h_count), (t, (h + h_count - 1) % h_count)
    after, before = ((t + 1) % t_count, h), ((t + t_count - 1) % t_count, h)
    routes = [("x", "y", "z"), ("y", "z", "x"), ("z", "x", "y")]
    peers = [later, earlier, after, before]
    for axis in AXES:
        for d in (1, 2, 3):
            for k in (0, 1):
                peers.append(device(moved(me, **{axis: d}, k=k)))
    peers.append(device(moved(me, k=1)))
    greet(peers)
    halo = []

    def neighbour(src, a, b, to):
        copy = pltpu.make_async_remote_copy(
            src_ref=src,
            dst_ref=window_ref.at[a, b],
            send_sem=halo_send_sem.at[len(halo)],
            recv_sem=halo_sem.at[len(halo)],
            device_id=to,
            device_id_type=MESH,
        )
        copy.start()
        halo.append(copy)

    neighbour(kv_ref, 1, 0, later)
    neighbour(kv_ref, 1, 2, earlier)
    neighbour(kv_ref, 0, 1, after)
    neighbour(kv_ref, 2, 1, before)
    for part in range(3):
        pltpu.make_async_copy(rows[part], rows[part], rows_sem.at[part]).wait()

    def pick(part, group):
        first, second, third = routes[part]

        @pl.loop(0, 4)
        def _(j):
            asker = {first: me[first], second: group, third: j}
            at = ((asker["z"] * 4 + asker["y"]) * 4 + asker["x"]) * 8
            for k in range(2):
                for holder in range(4):
                    for slot in range(4):
                        code = code_ref[part * 4 + holder, at + k * 512 + slot]
                        chosen[part][group, j, (k * 4 + holder) * 4 + slot] = rows[part][holder, code]

    middle = [[], [], []]

    def pass_on(part, n, d, copy):
        copy.wait()
        if d == 0:
            return
        second = routes[part][1]
        to = moved(me, **{second: d})
        sending = pltpu.make_async_remote_copy(
            src_ref=picked[part].at[to[second]],
            dst_ref=between[part].at[me[second]],
            send_sem=send_sem.at[part, 0],
            recv_sem=mid_sem.at[part, n],
            device_id=device(to),
            device_id_type=MESH,
        )
        sending.start()
        middle[part].append(sending)

    waiting = None
    for n, d in enumerate((1, 3, 2, 0)):
        for part in range(3):
            second = routes[part][1]
            group = moved(me, **{second: d})[second]
            pick(part, group)
            copy = pltpu.make_async_copy(
                chosen[part].at[group], picked[part].at[group], chosen_sem.at[part, n]
            )
            copy.start()
            if waiting is not None:
                pass_on(*waiting)
            waiting = (part, n, d, copy)
    pass_on(*waiting)
    for n, d in enumerate((0, 3, 1, 2)):
        if n == 1:
            for came, j in ((0, 0), (1, 2)):
                halo[came].wait_recv()
                neighbour(window_ref.at[1, j], 0, j, after)
                neighbour(window_ref.at[1, j], 2, j, before)
        for part in range(3):
            _, second, third = routes[part]
            came = moved(me, **{second: d})[second]
            if n > 0:
                middle[part][n - 1].wait_recv()
                held = between[part].at[came]
            else:
                held = picked[part].at[came]
            for e in (1, 3, 2, 0):
                for k in (0, 1):
                    to = moved(me, **{third: e}, k=k)
                    src = held.at[to[third], pl.ds(to["k"] * 16, 16)]
                    dst = got[part].at[came, me[third], me["k"]]
                    if e == 0 and k == 0:
                        pltpu.make_async_copy(src, dst, local_sem.at[part]).start()
                    else:
                        pltpu.make_async_remote_copy(
                            src_ref=src,
                            dst_ref=dst,
                            send_sem=send_sem.at[part, 1],
                            recv_sem=last_sem.at[part],
                            device_id=device(to),
                            device_id_type=MESH,
                        ).start()
    for copy in halo[2:]:
        copy.wait_recv()
    valid = []
    for a in (-1, 0, 1):
        for b in (-1, 0, 1):
            inside = (t + a >= 0) & (t + a < t_count) & (h + b >= 0) & (h + b < h_count)
            valid.append(inside.astype(jnp.int32))

    @pl.loop(0, HEADS // PAIR)
    def _(i):
        window_heads(i, valid, q_ref, kv_ref, window_ref, acc_ref, stat_ref)

    for copy in halo:
        copy.wait_send()
    for part in range(3):
        whole = got[part].at[:, :, :, 0:14]
        pltpu.make_async_copy(whole, whole, last_sem.at[part]).wait()
        pltpu.make_async_copy(whole, whole, send_sem.at[part, 1]).wait()
        some = got[part].at[:, 0, 0]
        pltpu.make_async_copy(some, some, local_sem.at[part]).wait()
        some = between[part].at[0:3]
        pltpu.make_async_copy(some, some, send_sem.at[part, 0]).wait()


def exchange(codes, rows, kv, queries):
    hbm = pl.BlockSpec(memory_space=pl.ANY)
    vmem = pl.BlockSpec(memory_space=pltpu.VMEM)
    smem = pl.BlockSpec(memory_space=pltpu.SMEM)
    got = [jax.ShapeDtypeStruct((4, 4, 2, 16, r, HEAD_DIM), kv.dtype) for r in PART_ROWS]
    picked = [jax.ShapeDtypeStruct((4, 4, 32, r, HEAD_DIM), kv.dtype) for r in PART_ROWS]
    stat = jax.ShapeDtypeStruct((HEADS, ROWS, HEAD_DIM), jnp.float32)
    outs = pl.pallas_call(
        exchange_kernel,
        name="exchange",
        out_shape=got + picked + picked + [stat, stat],
        in_specs=[smem] + [hbm] * 3 + [vmem] * 2,
        out_specs=[hbm] * 9 + [vmem] * 2,
        scratch_shapes=[
            pltpu.VMEM((3, 3) + kv.shape, kv.dtype),
            *[pltpu.VMEM((4, NW * HEADS, r, HEAD_DIM), kv.dtype) for r in PART_ROWS],
            *[pltpu.VMEM(p.shape, p.dtype) for p in picked],
            pltpu.SemaphoreType.DMA((3,)),
            pltpu.SemaphoreType.DMA((3, 2)),
            pltpu.SemaphoreType.DMA((3, 3)),
            pltpu.SemaphoreType.DMA((3,)),
            pltpu.SemaphoreType.DMA((8,)),
            pltpu.SemaphoreType.DMA((8,)),
            pltpu.SemaphoreType.DMA((3,)),
            pltpu.SemaphoreType.DMA((3, 4)),
        ],
        compiler_params=pltpu.CompilerParams(
            collective_id=1, has_side_effects=True, vmem_limit_bytes=60 * 1024 * 1024
        ),
    )(codes, *rows, kv, queries)
    tiles = [g.reshape(SLOTS, r, HEAD_DIM) for g, r in zip(outs[:3], PART_ROWS)]
    return tiles, outs[9], outs[10]


def asked_codes(tables):
    at = position()
    holder = jnp.arange(4, dtype=jnp.int32)
    column = at["y"] * 32 + at["k"] * 16 + at["z"] * 4 + at["x"]
    columns = jnp.concatenate(
        [
            column + (holder - at["x"]),
            column + (holder - at["y"]) * 32,
            column + (holder - at["z"]) * 4,
        ]
    )
    mine = columns[:, None] == jnp.arange(tables.shape[-1], dtype=jnp.int32)
    asked = lax.dot_general(
        mine.astype(jnp.bfloat16),
        tables.reshape(-1, tables.shape[-1]).astype(jnp.bfloat16),
        (((1,), (1,)), ((), ())),
        preferred_element_type=jnp.float32,
    )
    return asked.astype(jnp.int32)


def far_kernel(
    slot_ref, q_ref, tiles0, tiles1, tiles2, acc_ref, stat_ref, w_ref, out_ref, total
):
    step = pl.program_id(0)
    steps = pl.num_programs(0)

    @pl.when(step == 0)
    def _():
        total[...] = jnp.zeros_like(total)

    heads = []
    for p in range(PAIR):
        cubes = []
        for c in range(NW):
            rows = slice(c * CUBE, (c + 1) * CUBE)
            query = q_ref[rows, p * HEAD_DIM : (p + 1) * HEAD_DIM]
            keys, values = [], []
            for f in range(FAR):
                slot = slot_ref[(c * HEADS + step * PAIR + p) * FAR + f]
                in0, in1, in2 = slot & (SLOTS - 1), (slot >> 9) & (SLOTS - 1), slot >> 18
                keys += [tiles0[in0], tiles1[in1, 0:16]]
                values += [tiles1[in1, 16:48], tiles2[in2]]
            keys = jnp.concatenate(keys, axis=0)
            values = jnp.concatenate(values, axis=0)
            scores = lax.dot_general(
                query, keys, (((1,), (1,)), ((), ())), preferred_element_type=jnp.float32
            )
            near_max = stat_ref[p, rows, 0:1]
            near_sum = stat_ref[p, rows, HEAD_DIM // 2 : HEAD_DIM // 2 + 1]
            largest = jnp.maximum(near_max, jnp.max(scores, axis=-1, keepdims=True))
            lifted = jnp.exp2((scores - largest) * EXP2_SCALE)
            fade = jnp.exp2((near_max - largest) * EXP2_SCALE)
            weight = near_sum * fade + jnp.sum(lifted, axis=-1, keepdims=True)
            summed = acc_ref[p, rows] * fade + jnp.dot(
                lifted.astype(jnp.bfloat16), values, preferred_element_type=jnp.float32
            )
            cubes.append((summed / weight).astype(jnp.bfloat16))
        heads.append(jnp.concatenate(cubes, axis=0))
    attended = jnp.concatenate(heads, axis=1)
    total[...] += jnp.dot(attended, w_ref[...], preferred_element_type=jnp.float32)

    @pl.when(step == steps - 1)
    def _():
        out_ref[...] = total[...].astype(out_ref.dtype)


def far_attention(far_slot, queries, tiles, acc, stat, out_weight):
    steps = HEADS // PAIR
    width = PAIR * HEAD_DIM
    model = queries.shape[1]
    near = pl.BlockSpec((PAIR, ROWS, HEAD_DIM), lambda i, s: (i, 0, 0))
    return pl.pallas_call(
        far_kernel,
        name="far_attention",
        out_shape=jax.ShapeDtypeStruct((ROWS, model), queries.dtype),
        grid_spec=pltpu.PrefetchScalarGridSpec(
            num_scalar_prefetch=1,
            grid=(steps,),
            in_specs=[
                pl.BlockSpec((ROWS, width), lambda i, s: (0, i)),
                *[
                    pl.BlockSpec(x.shape, lambda i, s: (0, 0, 0), pipeline_mode=pl.Buffered(1))
                    for x in tiles
                ],
                near,
                near,
                pl.BlockSpec((width, model), lambda i, s: (i, 0)),
            ],
            out_specs=pl.BlockSpec((ROWS, model), lambda i, s: (0, 0)),
            scratch_shapes=[pltpu.VMEM((ROWS, model), jnp.float32)],
        ),
        cost_estimate=pl.CostEstimate(
            flops=HEADS * 4 * ROWS * FAR * CUBE * HEAD_DIM + 2 * ROWS * model * model,
            bytes_accessed=50_000_000,
            transcendentals=HEADS * ROWS * FAR * CUBE,
        ),
    )(far_slot, queries, *tiles, acc, stat, out_weight)


def body(queries, keys_values, far_cubes, out_weight):
    tm_count = lax.axis_size("tm")
    height_count = lax.axis_size("height")
    device_count = tm_count * height_count
    model = queries.shape[-1]
    far = far_cubes.reshape(NW, HEADS, FAR)
    requests, far_slot = request_tables(far, device_count)
    kv = keys_values.reshape(NW, 2, CUBE, model)
    *rows, tables = spread(kv, requests)
    flat_queries = queries.reshape(ROWS, model)
    tiles, acc, stat = exchange(asked_codes(tables), rows, kv, flat_queries)
    output = far_attention(
        far_slot.reshape(NW * HEADS * FAR), flat_queries, tiles, acc, stat, out_weight
    )
    return output.reshape(queries.shape)


def solution(mesh):
    in_specs = (
        P("tm", "height", None, None, None),
        P("tm", "height", None, None, None, None),
        P("tm", "height", None, None, None),
        P(),
    )
    out_specs = P("tm", "height", None, None, None)
    return jax.shard_map(body, mesh=mesh, in_specs=in_specs, out_specs=out_specs, check_vma=False)
```

```python
import functools
import math

import jax
import jax.numpy as jnp
from jax import lax
from jax.experimental import pallas as pl
from jax.experimental.pallas import tpu as pltpu
from jax.sharding import PartitionSpec as P

HEADS = 24
HEAD_DIM = 128
CUBE = 64
FAR = 16
NW = 2
SLOTS = 512
PAIR = 2
GROUP = 4
ROWS = NW * CUBE
NEG = -1e30
EXP2_SCALE = math.log2(math.e) / math.sqrt(HEAD_DIM)


def request_tables(far, device_count):
    capacity = SLOTS // device_count
    cubes = device_count * NW
    hit = far[:, :, :, None] == jnp.arange(cubes, dtype=jnp.int32)
    wanted = jnp.any(hit, axis=(0, 2))
    wanted = jnp.transpose(wanted.reshape(HEADS, device_count, NW), (1, 2, 0))
    wanted = wanted.reshape(device_count, NW * HEADS)
    codes = jnp.arange(NW * HEADS, dtype=jnp.int32)
    before = (codes[:, None] < codes[None, :]).astype(jnp.bfloat16)
    rank = jnp.dot(wanted.astype(jnp.bfloat16), before, preferred_element_type=jnp.float32)
    rank = rank.astype(jnp.int32)
    chosen = wanted[:, :, None] & (rank[:, :, None] == jnp.arange(2 * capacity, dtype=jnp.int32))
    requests = jnp.sum(jnp.where(chosen, codes[None, :, None], 0), axis=1)
    slot = rank + jnp.arange(device_count, dtype=jnp.int32)[:, None] * capacity
    slot = jnp.transpose(slot.reshape(device_count, NW, HEADS), (2, 0, 1)).reshape(HEADS, cubes)
    far_slot = jnp.sum(jnp.where(hit, slot[None, :, None, :], 0), axis=-1)
    rank, owner = far_slot % capacity, far_slot // capacity
    y, k, z, x = owner // 32, owner // 16 % 2, owner // 4 % 4, owner % 4
    in_x = (((y * 4 + z) * 2 + k) * 4 + x) * capacity + rank
    in_y = (((z * 4 + x) * 2 + k) * 4 + y) * capacity + rank
    in_z = (((x * 4 + y) * 2 + k) * 4 + z) * capacity + rank
    return requests.T, in_x + in_y * SLOTS + in_z * SLOTS * SLOTS


PART_ROWS = (48, 64, 16)
PIECES = (
    ((0, 0, 48, 0),),
    ((0, 48, 64, 0), (1, 0, 48, 16)),
    ((1, 48, 64, 0),),
)
AXES = ("x", "y", "z")
MESH = pl.DeviceIdType.MESH


def position():
    t, h = lax.axis_index("tm"), lax.axis_index("height")
    return {"x": h % 4, "y": t // 2, "z": h // 4, "k": t % 2}


def device(at):
    return at["y"] * 2 + at["k"], at["z"] * 4 + at["x"]


def moved(at, **by):
    return {n: (v + by.get(n, 0)) % (2 if n == "k" else 4) for n, v in at.items()}


def greet(peers):
    barrier = pltpu.get_barrier_semaphore()
    for peer in peers:
        pl.semaphore_signal(barrier, inc=1, device_id=peer, device_id_type=MESH)
    pl.semaphore_wait(barrier, len(peers))


def spread_kernel(
    kv_ref,
    table_ref,
    rows0_ref,
    rows1_ref,
    rows2_ref,
    tables_ref,
    local_sem,
    send_sem,
    rows_sem,
    table_sem,
):
    me = position()
    rows_refs = (rows0_ref, rows1_ref, rows2_ref)
    peers = [device(moved(me, **{a: d})) for a in AXES for d in (1, 2, 3)]
    peers += [device(moved(me, k=1))]
    greet(peers)
    sent = []

    def send(src, dst, sem, to):
        copy = pltpu.make_async_remote_copy(
            src_ref=src,
            dst_ref=dst,
            send_sem=send_sem.at[len(sent)],
            recv_sem=sem,
            device_id=to,
            device_id_type=MESH,
        )
        copy.start()
        sent.append(copy)
        return copy

    own_table = tables_ref.at[me["k"], me["z"], me["y"], me["x"]]
    copies = [pltpu.make_async_copy(table_ref, own_table, local_sem.at[0])]
    for part in range(3):
        for n, (kind, low, high, at) in enumerate(PIECES[part]):
            copies.append(
                pltpu.make_async_copy(
                    kv_ref.at[:, kind, low:high],
                    rows_refs[part].at[me[AXES[part]], :, at : at + high - low],
                    local_sem.at[1 + part * 2 + n],
                )
            )
    for copy in copies:
        copy.start()

    def tables(stage, src, dst):
        axis = "xyzk"[stage]
        return [
            send(src, dst, table_sem.at[stage, d - 1], device(moved(me, **{axis: d})))
            for d in range(1, 2 if axis == "k" else 4)
        ]

    def nearest(part):
        groups = []
        for way, d in enumerate((1, 3)):
            group = []
            for n, (kind, low, high, at) in enumerate(PIECES[part]):
                group.append(
                    send(
                        kv_ref.at[:, kind, low:high],
                        rows_refs[part].at[me[AXES[part]], :, at : at + high - low],
                        rows_sem.at[part, way, n],
                        device(moved(me, **{AXES[part]: d})),
                    )
                )
            groups.append(group)
        return groups

    table_x = tables(0, table_ref, own_table)
    near = [nearest(0)]
    copies[0].wait()
    for copy in table_x:
        copy.wait_recv()
    row = tables_ref.at[me["k"], me["z"], me["y"]]
    table_y = tables(1, row, row)
    near.append(nearest(1))
    for copy in table_y:
        copy.wait_recv()
    plane = tables_ref.at[me["k"], me["z"]]
    table_z = tables(2, plane, plane)
    near.append(nearest(2))
    for copy in table_z:
        copy.wait_recv()
    core = tables_ref.at[me["k"]]
    table_k = tables(3, core, core)
    far = []
    for part in (0, 1, 2):
        for way, d in enumerate((1, 3)):
            for copy in near[part][way]:
                copy.wait_recv()
            block = rows_refs[part].at[moved(me, **{AXES[part]: 4 - d})[AXES[part]], way]
            far.append(
                send(
                    block,
                    block,
                    rows_sem.at[part, 2 + way, 0],
                    device(moved(me, **{AXES[part]: d})),
                )
            )
    for copy in table_k + far:
        copy.wait_recv()
    for copy in copies[1:]:
        copy.wait()
    for copy in sent:
        copy.wait_send()


def spread(kv, table):
    width = kv.shape[-1]
    hbm = pl.BlockSpec(memory_space=pl.ANY)
    vmem = pl.BlockSpec(memory_space=pltpu.VMEM)
    rows = [jax.ShapeDtypeStruct((4, NW, r, width), kv.dtype) for r in PART_ROWS]
    return pl.pallas_call(
        spread_kernel,
        name="spread",
        out_shape=(
            *rows,
            jax.ShapeDtypeStruct((2, 4, 4, 4) + table.shape, table.dtype),
        ),
        in_specs=[vmem, vmem],
        out_specs=(hbm,) * 4,
        scratch_shapes=[
            pltpu.SemaphoreType.DMA((7,)),
            pltpu.SemaphoreType.DMA((32,)),
            pltpu.SemaphoreType.DMA((3, 4, 2)),
            pltpu.SemaphoreType.DMA((4, 3)),
        ],
        compiler_params=pltpu.CompilerParams(collective_id=0, has_side_effects=True),
    )(kv, table)


def window_heads(i, valid, q_ref, own_ref, window_ref, acc_ref, stat_ref):
    def block(j, kind, lanes):
        ref = own_ref if j == 4 else window_ref.at[j // 3, j % 3]
        return ref[:, kind, :, lanes].reshape(ROWS, HEAD_DIM)

    for p in range(PAIR):
        head = i * PAIR + p
        lanes = pl.ds(pl.multiple_of(head * HEAD_DIM, HEAD_DIM), HEAD_DIM)
        query = q_ref[:, lanes]
        parts = []
        for j in range(9):
            keys = block(j, 0, lanes)
            score = lax.dot_general(
                query, keys, (((1,), (1,)), ((), ())), preferred_element_type=jnp.float32
            )
            parts.append(jnp.where(valid[j] > 0, score, NEG))
        scores = jnp.concatenate(parts, axis=-1)
        largest = jnp.max(scores, axis=-1, keepdims=True)
        lifted = jnp.exp2((scores - largest) * EXP2_SCALE)
        total = jnp.sum(lifted, axis=-1, keepdims=True)
        values = jnp.concatenate([block(j, 1, lanes) for j in range(9)], axis=0)
        acc_ref[head] = jnp.dot(
            lifted.astype(jnp.bfloat16), values, preferred_element_type=jnp.float32
        )
        lane = lax.broadcasted_iota(jnp.int32, (ROWS, HEAD_DIM), 1)
        stat_ref[head] = jnp.where(lane < HEAD_DIM // 2, largest, total)


def exchange_kernel(*refs):
    code_ref, rows_refs, (kv_ref, q_ref) = refs[0], refs[1:4], refs[4:6]
    got, between, picked, (acc_ref, stat_ref) = refs[6:9], refs[9:12], refs[12:15], refs[15:17]
    window_ref, rows, chosen = refs[17], refs[18:21], refs[21:24]
    local_sem, send_sem, mid_sem, last_sem, halo_send_sem, halo_sem, rows_sem, chosen_sem = refs[24:]
    for part in range(3):
        for code in range(NW * HEADS):
            lane = code % HEADS * HEAD_DIM
            pltpu.make_async_copy(
                rows_refs[part].at[:, code // HEADS, :, lane : lane + HEAD_DIM],
                rows[part].at[:, code],
                rows_sem.at[part],
            ).start()
    me = position()
    t, h = lax.axis_index("tm"), lax.axis_index("height")
    t_count, h_count = lax.axis_size("tm"), lax.axis_size("height")
    later, earlier = (t, (h + 1) % h_count), (t, (h + h_count - 1) % h_count)
    after, before = ((t + 1) % t_count, h), ((t + t_count - 1) % t_count, h)
    routes = [("x", "y", "z"), ("y", "z", "x"), ("z", "x", "y")]
    peers = [later, earlier, after, before]
    for axis in AXES:
        for d in (1, 2, 3):
            for k in (0, 1):
                peers.append(device(moved(me, **{axis: d}, k=k)))
    peers.append(device(moved(me, k=1)))
    greet(peers)
    halo = []

    def neighbour(src, a, b, to):
        copy = pltpu.make_async_remote_copy(
            src_ref=src,
            dst_ref=window_ref.at[a, b],
            send_sem=halo_send_sem.at[len(halo)],
            recv_sem=halo_sem.at[len(halo)],
            device_id=to,
            device_id_type=MESH,
        )
        copy.start()
        halo.append(copy)

    neighbour(kv_ref, 1, 0, later)
    neighbour(kv_ref, 1, 2, earlier)
    neighbour(kv_ref, 0, 1, after)
    neighbour(kv_ref, 2, 1, before)
    for part in range(3):
        pltpu.make_async_copy(rows[part], rows[part], rows_sem.at[part]).wait()

    def pick(part, group):
        first, second, third = routes[part]

        @pl.loop(0, 4)
        def _(j):
            asker = {first: me[first], second: group, third: j}
            at = ((asker["z"] * 4 + asker["y"]) * 4 + asker["x"]) * 8
            for k in range(2):
                for holder in range(4):
                    for slot in range(4):
                        code = code_ref[part * 4 + holder, at + k * 512 + slot]
                        chosen[part][group, j, (k * 4 + holder) * 4 + slot] = rows[part][holder, code]

    middle = [[], [], []]

    def pass_on(part, n, d, copy):
        copy.wait()
        if d == 0:
            return
        second = routes[part][1]
        to = moved(me, **{second: d})
        sending = pltpu.make_async_remote_copy(
            src_ref=picked[part].at[to[second]],
            dst_ref=between[part].at[me[second]],
            send_sem=send_sem.at[part, 0],
            recv_sem=mid_sem.at[part, n],
            device_id=device(to),
            device_id_type=MESH,
        )
        sending.start()
        middle[part].append(sending)

    waiting = None
    for n, d in enumerate((1, 3, 2, 0)):
        for part in range(3):
            second = routes[part][1]
            group = moved(me, **{second: d})[second]
            pick(part, group)
            copy = pltpu.make_async_copy(
                chosen[part].at[group], picked[part].at[group], chosen_sem.at[part, n]
            )
            copy.start()
            if waiting is not None:
                pass_on(*waiting)
            waiting = (part, n, d, copy)
    pass_on(*waiting)
    for n, d in enumerate((0, 3, 1, 2)):
        if n == 1:
            for came, j in ((0, 0), (1, 2)):
                halo[came].wait_recv()
                neighbour(window_ref.at[1, j], 0, j, after)
                neighbour(window_ref.at[1, j], 2, j, before)
        for part in range(3):
            _, second, third = routes[part]
            came = moved(me, **{second: d})[second]
            if n > 0:
                middle[part][n - 1].wait_recv()
                held = between[part].at[came]
            else:
                held = picked[part].at[came]
            for e in (1, 3, 2, 0):
                for k in (0, 1):
                    to = moved(me, **{third: e}, k=k)
                    src = held.at[to[third], pl.ds(to["k"] * 16, 16)]
                    dst = got[part].at[came, me[third], me["k"]]
                    if e == 0 and k == 0:
                        pltpu.make_async_copy(src, dst, local_sem.at[part]).start()
                    else:
                        pltpu.make_async_remote_copy(
                            src_ref=src,
                            dst_ref=dst,
                            send_sem=send_sem.at[part, 1],
                            recv_sem=last_sem.at[part],
                            device_id=device(to),
                            device_id_type=MESH,
                        ).start()
    for copy in halo[2:]:
        copy.wait_recv()
    valid = []
    for a in (-1, 0, 1):
        for b in (-1, 0, 1):
            inside = (t + a >= 0) & (t + a < t_count) & (h + b >= 0) & (h + b < h_count)
            valid.append(inside.astype(jnp.int32))

    @pl.loop(0, HEADS // PAIR)
    def _(i):
        window_heads(i, valid, q_ref, kv_ref, window_ref, acc_ref, stat_ref)

    for copy in halo:
        copy.wait_send()
    for part in range(3):
        whole = got[part].at[:, :, :, 0:14]
        pltpu.make_async_copy(whole, whole, last_sem.at[part]).wait()
        pltpu.make_async_copy(whole, whole, send_sem.at[part, 1]).wait()
        some = got[part].at[:, 0, 0]
        pltpu.make_async_copy(some, some, local_sem.at[part]).wait()
        some = between[part].at[0:3]
        pltpu.make_async_copy(some, some, send_sem.at[part, 0]).wait()


def exchange(codes, rows, kv, queries):
    hbm = pl.BlockSpec(memory_space=pl.ANY)
    vmem = pl.BlockSpec(memory_space=pltpu.VMEM)
    smem = pl.BlockSpec(memory_space=pltpu.SMEM)
    got = [jax.ShapeDtypeStruct((4, 4, 2, 16, r, HEAD_DIM), kv.dtype) for r in PART_ROWS]
    picked = [jax.ShapeDtypeStruct((4, 4, 32, r, HEAD_DIM), kv.dtype) for r in PART_ROWS]
    stat = jax.ShapeDtypeStruct((HEADS, ROWS, HEAD_DIM), jnp.float32)
    outs = pl.pallas_call(
        exchange_kernel,
        name="exchange",
        out_shape=got + picked + picked + [stat, stat],
        in_specs=[smem] + [hbm] * 3 + [vmem] * 2,
        out_specs=[hbm] * 9 + [vmem] * 2,
        scratch_shapes=[
            pltpu.VMEM((3, 3) + kv.shape, kv.dtype),
            *[pltpu.VMEM((4, NW * HEADS, r, HEAD_DIM), kv.dtype) for r in PART_ROWS],
            *[pltpu.VMEM(p.shape, p.dtype) for p in picked],
            pltpu.SemaphoreType.DMA((3,)),
            pltpu.SemaphoreType.DMA((3, 2)),
            pltpu.SemaphoreType.DMA((3, 3)),
            pltpu.SemaphoreType.DMA((3,)),
            pltpu.SemaphoreType.DMA((8,)),
            pltpu.SemaphoreType.DMA((8,)),
            pltpu.SemaphoreType.DMA((3,)),
            pltpu.SemaphoreType.DMA((3, 4)),
        ],
        compiler_params=pltpu.CompilerParams(
            collective_id=1, has_side_effects=True, vmem_limit_bytes=60 * 1024 * 1024
        ),
    )(codes, *rows, kv, queries)
    tiles = [g.reshape(SLOTS, r, HEAD_DIM) for g, r in zip(outs[:3], PART_ROWS)]
    return tiles, outs[9], outs[10]


def asked_codes(tables):
    at = position()
    holder = jnp.arange(4, dtype=jnp.int32)
    column = at["y"] * 32 + at["k"] * 16 + at["z"] * 4 + at["x"]
    columns = jnp.concatenate(
        [
            column + (holder - at["x"]),
            column + (holder - at["y"]) * 32,
            column + (holder - at["z"]) * 4,
        ]
    )
    mine = columns[:, None] == jnp.arange(tables.shape[-1], dtype=jnp.int32)
    asked = lax.dot_general(
        mine.astype(jnp.bfloat16),
        tables.reshape(-1, tables.shape[-1]).astype(jnp.bfloat16),
        (((1,), (1,)), ((), ())),
        preferred_element_type=jnp.float32,
    )
    return asked.astype(jnp.int32)


def far_kernel(
    slot_ref, q_ref, tiles0, tiles1, tiles2, acc_ref, stat_ref, w_ref, out_ref, total
):
    step = pl.program_id(0)
    steps = pl.num_programs(0)

    @pl.when(step == 0)
    def _():
        total[...] = jnp.zeros_like(total)

    heads = []
    for p in range(GROUP):
        cubes = []
        for c in range(NW):
            rows = slice(c * CUBE, (c + 1) * CUBE)
            query = q_ref[rows, p * HEAD_DIM : (p + 1) * HEAD_DIM]
            keys, values = [], []
            for f in range(FAR):
                slot = slot_ref[(c * HEADS + step * GROUP + p) * FAR + f]
                in0, in1, in2 = slot & (SLOTS - 1), (slot >> 9) & (SLOTS - 1), slot >> 18
                keys += [tiles0[in0], tiles1[in1, 0:16]]
                values += [tiles1[in1, 16:64], tiles2[in2]]
            keys = jnp.concatenate(keys, axis=0)
            values = jnp.concatenate(values, axis=0)
            scores = lax.dot_general(
                query, keys, (((1,), (1,)), ((), ())), preferred_element_type=jnp.float32
            )
            near_max = stat_ref[p, rows, 0:1]
            near_sum = stat_ref[p, rows, HEAD_DIM // 2 : HEAD_DIM // 2 + 1]
            largest = jnp.maximum(near_max, jnp.max(scores, axis=-1, keepdims=True))
            lifted = jnp.exp2((scores - largest) * EXP2_SCALE)
            fade = jnp.exp2((near_max - largest) * EXP2_SCALE)
            weight = near_sum * fade + jnp.sum(lifted, axis=-1, keepdims=True)
            summed = acc_ref[p, rows] * fade + jnp.dot(
                lifted.astype(jnp.bfloat16), values, preferred_element_type=jnp.float32
            )
            cubes.append((summed / weight).astype(jnp.bfloat16))
        heads.append(jnp.concatenate(cubes, axis=0))
    attended = jnp.concatenate(heads, axis=1)
    total[...] += jnp.dot(attended, w_ref[...], preferred_element_type=jnp.float32)

    @pl.when(step == steps - 1)
    def _():
        out_ref[...] = total[...].astype(out_ref.dtype)


def far_attention(far_slot, queries, tiles, acc, stat, out_weight):
    steps = HEADS // GROUP
    width = GROUP * HEAD_DIM
    model = queries.shape[1]
    near = pl.BlockSpec((GROUP, ROWS, HEAD_DIM), lambda i, s: (i, 0, 0))
    return pl.pallas_call(
        far_kernel,
        name="far_attention",
        out_shape=jax.ShapeDtypeStruct((ROWS, model), queries.dtype),
        grid_spec=pltpu.PrefetchScalarGridSpec(
            num_scalar_prefetch=1,
            grid=(steps,),
            in_specs=[
                pl.BlockSpec((ROWS, width), lambda i, s: (0, i)),
                *[
                    pl.BlockSpec(x.shape, lambda i, s: (0, 0, 0), pipeline_mode=pl.Buffered(1))
                    for x in tiles
                ],
                near,
                near,
                pl.BlockSpec((width, model), lambda i, s: (i, 0)),
            ],
            out_specs=pl.BlockSpec((ROWS, model), lambda i, s: (0, 0)),
            scratch_shapes=[pltpu.VMEM((ROWS, model), jnp.float32)],
        ),
        cost_estimate=pl.CostEstimate(
            flops=HEADS * 4 * ROWS * FAR * CUBE * HEAD_DIM + 2 * ROWS * model * model,
            bytes_accessed=50_000_000,
            transcendentals=HEADS * ROWS * FAR * CUBE,
        ),
    )(far_slot, queries, *tiles, acc, stat, out_weight)


def body(queries, keys_values, far_cubes, out_weight):
    tm_count = lax.axis_size("tm")
    height_count = lax.axis_size("height")
    device_count = tm_count * height_count
    model = queries.shape[-1]
    far = far_cubes.reshape(NW, HEADS, FAR)
    requests, far_slot = request_tables(far, device_count)
    kv = keys_values.reshape(NW, 2, CUBE, model)
    *rows, tables = spread(kv, requests)
    flat_queries = queries.reshape(ROWS, model)
    tiles, acc, stat = exchange(asked_codes(tables), rows, kv, flat_queries)
    output = far_attention(
        far_slot.reshape(NW * HEADS * FAR), flat_queries, tiles, acc, stat, out_weight
    )
    return output.reshape(queries.shape)


def solution(mesh):
    in_specs = (
        P("tm", "height", None, None, None),
        P("tm", "height", None, None, None, None),
        P("tm", "height", None, None, None),
        P(),
    )
    out_specs = P("tm", "height", None, None, None)
    return jax.shard_map(body, mesh=mesh, in_specs=in_specs, out_specs=out_specs, check_vma=False)
```

```python
import functools
import math

import jax
import jax.numpy as jnp
from jax import lax
from jax.experimental import pallas as pl
from jax.experimental.pallas import tpu as pltpu
from jax.sharding import PartitionSpec as P

HEADS = 24
HEAD_DIM = 128
CUBE = 64
FAR = 16
NW = 2
SLOTS = 512
PAIR = 2
GROUP = 4
ROWS = NW * CUBE
NEG = -1e30
EXP2_SCALE = math.log2(math.e) / math.sqrt(HEAD_DIM)


def request_tables(far, device_count):
    capacity = SLOTS // device_count
    cubes = device_count * NW
    hit = far[:, :, :, None] == jnp.arange(cubes, dtype=jnp.int32)
    wanted = jnp.any(hit, axis=(0, 2))
    wanted = jnp.transpose(wanted.reshape(HEADS, device_count, NW), (1, 2, 0))
    wanted = wanted.reshape(device_count, NW * HEADS)
    codes = jnp.arange(NW * HEADS, dtype=jnp.int32)
    before = (codes[:, None] < codes[None, :]).astype(jnp.bfloat16)
    rank = jnp.dot(wanted.astype(jnp.bfloat16), before, preferred_element_type=jnp.float32)
    rank = rank.astype(jnp.int32)
    chosen = wanted[:, :, None] & (rank[:, :, None] == jnp.arange(2 * capacity, dtype=jnp.int32))
    requests = jnp.sum(jnp.where(chosen, codes[None, :, None], 0), axis=1)
    slot = rank + jnp.arange(device_count, dtype=jnp.int32)[:, None] * capacity
    slot = jnp.transpose(slot.reshape(device_count, NW, HEADS), (2, 0, 1)).reshape(HEADS, cubes)
    far_slot = jnp.sum(jnp.where(hit, slot[None, :, None, :], 0), axis=-1)
    rank, owner = far_slot % capacity, far_slot // capacity
    y, k, z, x = owner // 32, owner // 16 % 2, owner // 4 % 4, owner % 4
    in_x = (((y * 4 + z) * 2 + k) * 4 + x) * capacity + rank
    in_y = (((z * 4 + x) * 2 + k) * 4 + y) * capacity + rank
    in_z = (((x * 4 + y) * 2 + k) * 4 + z) * capacity + rank
    return requests.T, in_x + in_y * SLOTS + in_z * SLOTS * SLOTS


PART_ROWS = (48, 48, 32)
PIECES = (
    ((0, 0, 48, 0),),
    ((0, 48, 64, 0), (1, 0, 32, 16)),
    ((1, 32, 64, 0),),
)
AXES = ("x", "y", "z")
MESH = pl.DeviceIdType.MESH


def position():
    t, h = lax.axis_index("tm"), lax.axis_index("height")
    return {"x": h % 4, "y": t // 2, "z": h // 4, "k": t % 2}


def device(at):
    return at["y"] * 2 + at["k"], at["z"] * 4 + at["x"]


def moved(at, **by):
    return {n: (v + by.get(n, 0)) % (2 if n == "k" else 4) for n, v in at.items()}


def greet(peers):
    barrier = pltpu.get_barrier_semaphore()
    for peer in peers:
        pl.semaphore_signal(barrier, inc=1, device_id=peer, device_id_type=MESH)
    pl.semaphore_wait(barrier, len(peers))


def spread_kernel(
    kv_ref,
    table_ref,
    rows0_ref,
    rows1_ref,
    rows2_ref,
    tables_ref,
    local_sem,
    send_sem,
    rows_sem,
    table_sem,
):
    me = position()
    rows_refs = (rows0_ref, rows1_ref, rows2_ref)
    peers = [device(moved(me, **{a: d})) for a in AXES for d in (1, 2, 3)]
    peers += [device(moved(me, k=1))]
    greet(peers)
    sent = []

    def send(src, dst, sem, to):
        copy = pltpu.make_async_remote_copy(
            src_ref=src,
            dst_ref=dst,
            send_sem=send_sem.at[len(sent)],
            recv_sem=sem,
            device_id=to,
            device_id_type=MESH,
        )
        copy.start()
        sent.append(copy)
        return copy

    own_table = tables_ref.at[me["k"], me["z"], me["y"], me["x"]]
    copies = [pltpu.make_async_copy(table_ref, own_table, local_sem.at[0])]
    for part in range(3):
        for n, (kind, low, high, at) in enumerate(PIECES[part]):
            copies.append(
                pltpu.make_async_copy(
                    kv_ref.at[:, kind, low:high],
                    rows_refs[part].at[me[AXES[part]], :, at : at + high - low],
                    local_sem.at[1 + part * 2 + n],
                )
            )
    for copy in copies:
        copy.start()

    def tables(stage, src, dst):
        axis = "xyzk"[stage]
        return [
            send(src, dst, table_sem.at[stage, d - 1], device(moved(me, **{axis: d})))
            for d in range(1, 2 if axis == "k" else 4)
        ]

    def nearest(part):
        groups = []
        for way, d in enumerate((1, 3)):
            group = []
            for n, (kind, low, high, at) in enumerate(PIECES[part]):
                group.append(
                    send(
                        kv_ref.at[:, kind, low:high],
                        rows_refs[part].at[me[AXES[part]], :, at : at + high - low],
                        rows_sem.at[part, way, n],
                        device(moved(me, **{AXES[part]: d})),
                    )
                )
            groups.append(group)
        return groups

    table_x = tables(0, table_ref, own_table)
    near = [nearest(0)]
    copies[0].wait()
    for copy in table_x:
        copy.wait_recv()
    row = tables_ref.at[me["k"], me["z"], me["y"]]
    table_y = tables(1, row, row)
    near.append(nearest(1))
    for copy in table_y:
        copy.wait_recv()
    plane = tables_ref.at[me["k"], me["z"]]
    table_z = tables(2, plane, plane)
    near.append(nearest(2))
    for copy in table_z:
        copy.wait_recv()
    core = tables_ref.at[me["k"]]
    table_k = tables(3, core, core)
    far = []
    for part in (0, 1, 2):
        for way, d in enumerate((1, 3)):
            for copy in near[part][way]:
                copy.wait_recv()
            block = rows_refs[part].at[moved(me, **{AXES[part]: 4 - d})[AXES[part]], way]
            far.append(
                send(
                    block,
                    block,
                    rows_sem.at[part, 2 + way, 0],
                    device(moved(me, **{AXES[part]: d})),
                )
            )
    for copy in table_k + far:
        copy.wait_recv()
    for copy in copies[1:]:
        copy.wait()
    for copy in sent:
        copy.wait_send()


def spread(kv, table):
    width = kv.shape[-1]
    hbm = pl.BlockSpec(memory_space=pl.ANY)
    vmem = pl.BlockSpec(memory_space=pltpu.VMEM)
    rows = [jax.ShapeDtypeStruct((4, NW, r, width), kv.dtype) for r in PART_ROWS]
    return pl.pallas_call(
        spread_kernel,
        name="spread",
        out_shape=(
            *rows,
            jax.ShapeDtypeStruct((2, 4, 4, 4) + table.shape, table.dtype),
        ),
        in_specs=[vmem, vmem],
        out_specs=(hbm,) * 4,
        scratch_shapes=[
            pltpu.SemaphoreType.DMA((7,)),
            pltpu.SemaphoreType.DMA((32,)),
            pltpu.SemaphoreType.DMA((3, 4, 2)),
            pltpu.SemaphoreType.DMA((4, 3)),
        ],
        compiler_params=pltpu.CompilerParams(collective_id=0, has_side_effects=True),
    )(kv, table)


def window_heads(i, valid, q_ref, own_ref, window_ref, acc_ref, stat_ref):
    def block(j, kind, lanes):
        ref = own_ref if j == 4 else window_ref.at[j // 3, j % 3]
        return ref[:, kind, :, lanes].reshape(ROWS, HEAD_DIM)

    for p in range(PAIR):
        head = i * PAIR + p
        lanes = pl.ds(pl.multiple_of(head * HEAD_DIM, HEAD_DIM), HEAD_DIM)
        query = q_ref[:, lanes]
        parts = []
        for j in range(9):
            keys = block(j, 0, lanes)
            score = lax.dot_general(
                query, keys, (((1,), (1,)), ((), ())), preferred_element_type=jnp.float32
            )
            parts.append(jnp.where(valid[j] > 0, score, NEG))
        scores = jnp.concatenate(parts, axis=-1)
        largest = jnp.max(scores, axis=-1, keepdims=True)
        lifted = jnp.exp2((scores - largest) * EXP2_SCALE)
        total = jnp.sum(lifted, axis=-1, keepdims=True)
        values = jnp.concatenate([block(j, 1, lanes) for j in range(9)], axis=0)
        acc_ref[head] = jnp.dot(
            lifted.astype(jnp.bfloat16), values, preferred_element_type=jnp.float32
        )
        lane = lax.broadcasted_iota(jnp.int32, (ROWS, HEAD_DIM), 1)
        stat_ref[head] = jnp.where(lane < HEAD_DIM // 2, largest, total)


def exchange_kernel(*refs):
    code_ref, rows_refs, (kv_ref, q_ref) = refs[0], refs[1:4], refs[4:6]
    got, between, picked, (acc_ref, stat_ref) = refs[6:9], refs[9:12], refs[12:15], refs[15:17]
    window_ref, rows, chosen = refs[17], refs[18:21], refs[21:24]
    local_sem, send_sem, mid_sem, last_sem, halo_send_sem, halo_sem, rows_sem, chosen_sem = refs[24:]
    for part in range(3):
        for code in range(NW * HEADS):
            lane = code % HEADS * HEAD_DIM
            pltpu.make_async_copy(
                rows_refs[part].at[:, code // HEADS, :, lane : lane + HEAD_DIM],
                rows[part].at[:, code],
                rows_sem.at[part],
            ).start()
    me = position()
    t, h = lax.axis_index("tm"), lax.axis_index("height")
    t_count, h_count = lax.axis_size("tm"), lax.axis_size("height")
    later, earlier = (t, (h + 1) % h_count), (t, (h + h_count - 1) % h_count)
    after, before = ((t + 1) % t_count, h), ((t + t_count - 1) % t_count, h)
    routes = [("x", "y", "z"), ("y", "z", "x"), ("z", "x", "y")]
    peers = [later, earlier, after, before]
    for axis in AXES:
        for d in (1, 2, 3):
            for k in (0, 1):
                peers.append(device(moved(me, **{axis: d}, k=k)))
    peers.append(device(moved(me, k=1)))
    greet(peers)
    halo = []

    def neighbour(src, a, b, to):
        copy = pltpu.make_async_remote_copy(
            src_ref=src,
            dst_ref=window_ref.at[a, b],
            send_sem=halo_send_sem.at[len(halo)],
            recv_sem=halo_sem.at[len(halo)],
            device_id=to,
            device_id_type=MESH,
        )
        copy.start()
        halo.append(copy)

    neighbour(kv_ref, 1, 0, later)
    neighbour(kv_ref, 1, 2, earlier)
    neighbour(kv_ref, 0, 1, after)
    neighbour(kv_ref, 2, 1, before)
    for part in range(3):
        pltpu.make_async_copy(rows[part], rows[part], rows_sem.at[part]).wait()

    def pick(part, group):
        first, second, third = routes[part]

        @pl.loop(0, 4)
        def _(j):
            asker = {first: me[first], second: group, third: j}
            at = ((asker["z"] * 4 + asker["y"]) * 4 + asker["x"]) * 8
            for k in range(2):
                for holder in range(4):
                    for slot in range(4):
                        code = code_ref[part * 4 + holder, at + k * 512 + slot]
                        chosen[part][group, j, (k * 4 + holder) * 4 + slot] = rows[part][holder, code]

    middle = [[], [], []]

    def pass_on(part, n, d, copy):
        copy.wait()
        if d == 0:
            return
        second = routes[part][1]
        to = moved(me, **{second: d})
        sending = pltpu.make_async_remote_copy(
            src_ref=picked[part].at[to[second]],
            dst_ref=between[part].at[me[second]],
            send_sem=send_sem.at[part, 0],
            recv_sem=mid_sem.at[part, n],
            device_id=device(to),
            device_id_type=MESH,
        )
        sending.start()
        middle[part].append(sending)

    waiting = None
    for n, d in enumerate((1, 3, 2, 0)):
        for part in range(3):
            second = routes[part][1]
            group = moved(me, **{second: d})[second]
            pick(part, group)
            copy = pltpu.make_async_copy(
                chosen[part].at[group], picked[part].at[group], chosen_sem.at[part, n]
            )
            copy.start()
            if waiting is not None:
                pass_on(*waiting)
            waiting = (part, n, d, copy)
    pass_on(*waiting)
    for n, d in enumerate((0, 3, 1, 2)):
        if n == 1:
            for came, j in ((0, 0), (1, 2)):
                halo[came].wait_recv()
                neighbour(window_ref.at[1, j], 0, j, after)
                neighbour(window_ref.at[1, j], 2, j, before)
        for part in (1, 2, 0):
            _, second, third = routes[part]
            came = moved(me, **{second: d})[second]
            if n > 0:
                middle[part][n - 1].wait_recv()
                held = between[part].at[came]
            else:
                held = picked[part].at[came]
            for e in (1, 3, 2, 0):
                for k in (0, 1):
                    to = moved(me, **{third: e}, k=k)
                    src = held.at[to[third], pl.ds(to["k"] * 16, 16)]
                    dst = got[part].at[came, me[third], me["k"]]
                    if e == 0 and k == 0:
                        pltpu.make_async_copy(src, dst, local_sem.at[part]).start()
                    else:
                        pltpu.make_async_remote_copy(
                            src_ref=src,
                            dst_ref=dst,
                            send_sem=send_sem.at[part, 1],
                            recv_sem=last_sem.at[part],
                            device_id=device(to),
                            device_id_type=MESH,
                        ).start()
    for copy in halo[2:]:
        copy.wait_recv()
    valid = []
    for a in (-1, 0, 1):
        for b in (-1, 0, 1):
            inside = (t + a >= 0) & (t + a < t_count) & (h + b >= 0) & (h + b < h_count)
            valid.append(inside.astype(jnp.int32))

    @pl.loop(0, HEADS // PAIR)
    def _(i):
        window_heads(i, valid, q_ref, kv_ref, window_ref, acc_ref, stat_ref)

    for copy in halo:
        copy.wait_send()
    for part in range(3):
        whole = got[part].at[:, :, :, 0:14]
        pltpu.make_async_copy(whole, whole, last_sem.at[part]).wait()
        pltpu.make_async_copy(whole, whole, send_sem.at[part, 1]).wait()
        some = got[part].at[:, 0, 0]
        pltpu.make_async_copy(some, some, local_sem.at[part]).wait()
        some = between[part].at[0:3]
        pltpu.make_async_copy(some, some, send_sem.at[part, 0]).wait()


def exchange(codes, rows, kv, queries):
    hbm = pl.BlockSpec(memory_space=pl.ANY)
    vmem = pl.BlockSpec(memory_space=pltpu.VMEM)
    smem = pl.BlockSpec(memory_space=pltpu.SMEM)
    got = [jax.ShapeDtypeStruct((4, 4, 2, 16, r, HEAD_DIM), kv.dtype) for r in PART_ROWS]
    picked = [jax.ShapeDtypeStruct((4, 4, 32, r, HEAD_DIM), kv.dtype) for r in PART_ROWS]
    stat = jax.ShapeDtypeStruct((HEADS, ROWS, HEAD_DIM), jnp.float32)
    outs = pl.pallas_call(
        exchange_kernel,
        name="exchange",
        out_shape=got + picked + picked + [stat, stat],
        in_specs=[smem] + [hbm] * 3 + [vmem] * 2,
        out_specs=[hbm] * 9 + [vmem] * 2,
        scratch_shapes=[
            pltpu.VMEM((3, 3) + kv.shape, kv.dtype),
            *[pltpu.VMEM((4, NW * HEADS, r, HEAD_DIM), kv.dtype) for r in PART_ROWS],
            *[pltpu.VMEM(p.shape, p.dtype) for p in picked],
            pltpu.SemaphoreType.DMA((3,)),
            pltpu.SemaphoreType.DMA((3, 2)),
            pltpu.SemaphoreType.DMA((3, 3)),
            pltpu.SemaphoreType.DMA((3,)),
            pltpu.SemaphoreType.DMA((8,)),
            pltpu.SemaphoreType.DMA((8,)),
            pltpu.SemaphoreType.DMA((3,)),
            pltpu.SemaphoreType.DMA((3, 4)),
        ],
        compiler_params=pltpu.CompilerParams(
            collective_id=1, has_side_effects=True, vmem_limit_bytes=60 * 1024 * 1024
        ),
    )(codes, *rows, kv, queries)
    tiles = [g.reshape(SLOTS, r, HEAD_DIM) for g, r in zip(outs[:3], PART_ROWS)]
    return tiles, outs[9], outs[10]


def asked_codes(tables):
    at = position()
    holder = jnp.arange(4, dtype=jnp.int32)
    column = at["y"] * 32 + at["k"] * 16 + at["z"] * 4 + at["x"]
    columns = jnp.concatenate(
        [
            column + (holder - at["x"]),
            column + (holder - at["y"]) * 32,
            column + (holder - at["z"]) * 4,
        ]
    )
    mine = columns[:, None] == jnp.arange(tables.shape[-1], dtype=jnp.int32)
    asked = lax.dot_general(
        mine.astype(jnp.bfloat16),
        tables.reshape(-1, tables.shape[-1]).astype(jnp.bfloat16),
        (((1,), (1,)), ((), ())),
        preferred_element_type=jnp.float32,
    )
    return asked.astype(jnp.int32)


def far_kernel(
    slot_ref, q_ref, tiles0, tiles1, tiles2, acc_ref, stat_ref, w_ref, out_ref, total
):
    step = pl.program_id(0)
    steps = pl.num_programs(0)

    @pl.when(step == 0)
    def _():
        total[...] = jnp.zeros_like(total)

    heads = []
    for p in range(GROUP):
        cubes = []
        for c in range(NW):
            rows = slice(c * CUBE, (c + 1) * CUBE)
            query = q_ref[rows, p * HEAD_DIM : (p + 1) * HEAD_DIM]
            keys, values = [], []
            for f in range(FAR):
                slot = slot_ref[(c * HEADS + step * GROUP + p) * FAR + f]
                in0, in1, in2 = slot & (SLOTS - 1), (slot >> 9) & (SLOTS - 1), slot >> 18
                keys += [tiles0[in0], tiles1[in1, 0:16]]
                values += [tiles1[in1, 16:48], tiles2[in2]]
            keys = jnp.concatenate(keys, axis=0)
            values = jnp.concatenate(values, axis=0)
            scores = lax.dot_general(
                query, keys, (((1,), (1,)), ((), ())), preferred_element_type=jnp.float32
            )
            near_max = stat_ref[p, rows, 0:1]
            near_sum = stat_ref[p, rows, HEAD_DIM // 2 : HEAD_DIM // 2 + 1]
            largest = jnp.maximum(near_max, jnp.max(scores, axis=-1, keepdims=True))
            lifted = jnp.exp2((scores - largest) * EXP2_SCALE)
            fade = jnp.exp2((near_max - largest) * EXP2_SCALE)
            weight = near_sum * fade + jnp.sum(lifted, axis=-1, keepdims=True)
            summed = acc_ref[p, rows] * fade + jnp.dot(
                lifted.astype(jnp.bfloat16), values, preferred_element_type=jnp.float32
            )
            cubes.append((summed / weight).astype(jnp.bfloat16))
        heads.append(jnp.concatenate(cubes, axis=0))
    attended = jnp.concatenate(heads, axis=1)
    total[...] += jnp.dot(attended, w_ref[...], preferred_element_type=jnp.float32)

    @pl.when(step == steps - 1)
    def _():
        out_ref[...] = total[...].astype(out_ref.dtype)


def far_attention(far_slot, queries, tiles, acc, stat, out_weight):
    steps = HEADS // GROUP
    width = GROUP * HEAD_DIM
    model = queries.shape[1]
    near = pl.BlockSpec((GROUP, ROWS, HEAD_DIM), lambda i, s: (i, 0, 0))
    return pl.pallas_call(
        far_kernel,
        name="far_attention",
        out_shape=jax.ShapeDtypeStruct((ROWS, model), queries.dtype),
        grid_spec=pltpu.PrefetchScalarGridSpec(
            num_scalar_prefetch=1,
            grid=(steps,),
            in_specs=[
                pl.BlockSpec((ROWS, width), lambda i, s: (0, i)),
                *[
                    pl.BlockSpec(x.shape, lambda i, s: (0, 0, 0), pipeline_mode=pl.Buffered(1))
                    for x in tiles
                ],
                near,
                near,
                pl.BlockSpec((width, model), lambda i, s: (i, 0)),
            ],
            out_specs=pl.BlockSpec((ROWS, model), lambda i, s: (0, 0)),
            scratch_shapes=[pltpu.VMEM((ROWS, model), jnp.float32)],
        ),
        cost_estimate=pl.CostEstimate(
            flops=HEADS * 4 * ROWS * FAR * CUBE * HEAD_DIM + 2 * ROWS * model * model,
            bytes_accessed=50_000_000,
            transcendentals=HEADS * ROWS * FAR * CUBE,
        ),
    )(far_slot, queries, *tiles, acc, stat, out_weight)


def body(queries, keys_values, far_cubes, out_weight):
    tm_count = lax.axis_size("tm")
    height_count = lax.axis_size("height")
    device_count = tm_count * height_count
    model = queries.shape[-1]
    far = far_cubes.reshape(NW, HEADS, FAR)
    requests, far_slot = request_tables(far, device_count)
    kv = keys_values.reshape(NW, 2, CUBE, model)
    *rows, tables = spread(kv, requests)
    flat_queries = queries.reshape(ROWS, model)
    tiles, acc, stat = exchange(asked_codes(tables), rows, kv, flat_queries)
    output = far_attention(
        far_slot.reshape(NW * HEADS * FAR), flat_queries, tiles, acc, stat, out_weight
    )
    return output.reshape(queries.shape)


def solution(mesh):
    in_specs = (
        P("tm", "height", None, None, None),
        P("tm", "height", None, None, None, None),
        P("tm", "height", None, None, None),
        P(),
    )
    out_specs = P("tm", "height", None, None, None)
    return jax.shard_map(body, mesh=mesh, in_specs=in_specs, out_specs=out_specs, check_vma=False)
```
